256 devices in a mesh: box: 32 (over z, x_lo, core), face: 8 (over y, x_hi).
Axes of the slice: x: 4 (x_hi: 2, x_lo: 2; x = x_hi * 2 + x_lo), y: 4, z: 8, core: 2. Of those that a mesh axis runs over, the one named last changes fastest.
Arguments:
- leaf_maps: bfloat16 [2, 1, 32, 3, 512, 1536], P(None, None, 'box', None, 'face'), may hold values from -6 to 6
- w_first: bfloat16 [2, 1, 8192, 512], P(None, None, 'box'), may hold values from -0.01171875 to 0.01171875
- w_second: bfloat16 [2, 1, 4096, 512], P(None, None, 'box'), may hold values from -0.01171875 to 0.01171875
- skel_first: int32 [1, 16, 512], replicated, may hold values from 0 to 1023, as said below
- skel_second: int32 [1, 8, 512], replicated, may hold values from 0 to 1023, as said below
Outputs:
- grand_maps: bfloat16 [2, 1, 16384, 1536], P(None, None, ('box', 'face'))
The draws below stay inside these ranges and needn't reach their ends.
Inputs may be any that keep to these rules, and one draw needn't show every extreme that they name: `skel_first`: each row holds 512 distinct indices, 0 and 1023 among them. `skel_second`: each row holds 512 distinct indices, 0 and 1023 among them.
All inputs are finite; a program needn't handle non-finite values.
Results may differ from the reference program's by a relative error of at most 0.0075.
Values may be sent and summed in bfloat16 or wider, within the bound.
A program may use at most 64 MiB of HBM per device.

```python
import jax
import jax.numpy as jnp
from jax import lax

K = 512
TREES = 1
PARENTS = 16
GRANDS = 8
N_BOX = 32
N_FACE = 8


def skeleton_draw(base_key, count):
    block_len = K // N_FACE
    block_total = 2 * N_FACE
    whole_count = max(1, N_FACE // 2)
    rest_count = K - whole_count * block_len
    all_keys = jax.random.split(base_key, count)

    def one_row(row_key):
        src_key, dst_key, noise_key, inner_key, rest_key = jax.random.split(row_key, 5)
        src_order = jax.random.permutation(src_key, jnp.arange(block_total, dtype=jnp.int32))
        dst_order = jax.random.permutation(dst_key, jnp.arange(N_FACE, dtype=jnp.int32))
        whole_src = src_order[:whole_count]
        index_all = jnp.arange(2 * K, dtype=jnp.int32)
        in_whole = jnp.any((index_all // block_len)[:, None] == whole_src[None, :], axis=1)
        is_end = (index_all == 0) | (index_all == 2 * K - 1)
        noise = jax.random.permutation(noise_key, jnp.arange(2 * K, dtype=jnp.int32))
        score = noise + 2 * K * is_end.astype(jnp.int32) + 4 * K * in_whole.astype(jnp.int32)
        top_scores, chosen = lax.top_k(score, K)
        chosen = chosen.astype(jnp.int32)
        inner = jax.random.permutation(inner_key, jnp.arange(block_len, dtype=jnp.int32))
        whole_rows = whole_src[:, None] * block_len + inner[None, :]
        rest_rows = jax.random.permutation(rest_key, chosen[whole_count * block_len:])
        layout = jnp.zeros((N_FACE, block_len), jnp.int32)
        layout = layout.at[dst_order[:whole_count]].set(whole_rows)
        if rest_count > 0:
            layout = layout.at[dst_order[whole_count:]].set(rest_rows.reshape(N_FACE - whole_count, block_len))
        return layout.reshape(K)
    return jax.vmap(one_row)(all_keys)


def draw_skel_first(key, part):
    return skeleton_draw(jax.random.fold_in(key, 11), TREES * PARENTS).reshape(TREES, PARENTS, K)


def draw_skel_second(key, part):
    return skeleton_draw(jax.random.fold_in(key, 23), TREES * GRANDS).reshape(TREES, GRANDS, K)


def level_of(rng, shape, cuts, smallest, top_value):
    level, own = 1.0, jax.random.fold_in(rng, 6)
    for dim, shards_of in cuts:
        draws = jnp.exp(jax.random.uniform(jax.random.fold_in(own, dim), (shards_of,), jnp.float32, smallest / len(cuts), top_value / len(cuts)))
        level = level * jnp.repeat(draws, shape[dim] // shards_of).reshape([-1 if axis == dim else 1 for axis in range(len(shape))])
    return level


def scatter_about(own_key, shape, deviation, limit, pieces=(), kind=jnp.bfloat16):
    entries = jax.random.normal(own_key, shape, jnp.float32) * deviation
    if len(pieces) > 0:
        entries = level_of(own_key, shape, pieces, -0.22, 0.18) * entries
    return jnp.clip(entries, min=-limit, max=limit).astype(kind)


def setup_inputs(seed: int = 0) -> dict:
    splits = jax.random.split(jax.random.key(seed), 6)
    leaf_maps = scatter_about(splits[0], (2, TREES, N_BOX, 3, K, 3 * K), 1.0, 6.0, ((2, 32), (4, 8)))
    w_first = scatter_about(splits[1], (2, TREES, PARENTS * K, K), (K * K) ** -0.5, 0.01171875, ((2, 32),))
    w_second = scatter_about(splits[2], (2, TREES, GRANDS * K, K), (K * K) ** -0.5, 0.01171875, ((2, 32),))
    skel_first = draw_skel_first(jax.random.fold_in(splits[5], 71), 0)
    skel_second = draw_skel_second(jax.random.fold_in(splits[5], 71), 0)
    return {"leaf_maps": leaf_maps, "w_first": w_first, "w_second": w_second, "skel_first": skel_first, "skel_second": skel_second}


def complex_dot(left_op, right_op):
    left_op = left_op.astype(jnp.float32)
    right_op = right_op.astype(jnp.float32)

    def real_dot(first_op, second_op):
        return jnp.matmul(first_op, second_op, precision=lax.Precision.HIGHEST)

    real_part = real_dot(left_op[0], right_op[0]) - real_dot(left_op[1], right_op[1])
    imag_part = real_dot(left_op[0], right_op[1]) + real_dot(left_op[1], right_op[0])
    return jnp.stack([real_part, imag_part])


def merge_pair(left_map, right_map, weight_inv, skeleton, keep_rows):
    ext_left = jnp.concatenate([jnp.arange(K), jnp.arange(2 * K, 3 * K)]).astype(jnp.int32)
    int_left = jnp.arange(K, 2 * K).astype(jnp.int32)
    ext_right = jnp.concatenate([jnp.arange(2 * K, 3 * K), jnp.arange(K, 2 * K)]).astype(jnp.int32)
    int_right = jnp.arange(0, K).astype(jnp.int32)
    left_ext = jnp.take(left_map, ext_left, axis=1)
    right_ext = jnp.take(right_map, ext_right, axis=1)
    couple_rows = jnp.concatenate([jnp.take(left_ext, int_left, axis=2), jnp.take(right_ext, int_right, axis=2)], axis=1)
    iface_cols = jnp.concatenate([jnp.take(jnp.take(left_map, int_left, axis=1), ext_left, axis=2),
                                  jnp.take(jnp.take(right_map, int_right, axis=1), ext_right, axis=2)], axis=2)
    zero_block = jnp.zeros((2, 2 * K, 2 * K), left_map.dtype)
    block_diag = jnp.concatenate([
        jnp.concatenate([jnp.take(left_ext, ext_left, axis=2), zero_block], axis=2),
        jnp.concatenate([zero_block, jnp.take(right_ext, ext_right, axis=2)], axis=2)], axis=1)
    selected = jnp.concatenate([jnp.arange(K).astype(jnp.int32), jnp.arange(3 * K, 4 * K).astype(jnp.int32),
                                K + skeleton.astype(jnp.int32)])
    if keep_rows:
        couple_rows = jnp.take(couple_rows, selected, axis=1)
        block_diag = jnp.take(block_diag, selected, axis=1)
    hidden = complex_dot(couple_rows, weight_inv).astype(jnp.bfloat16)
    merged = jnp.take(block_diag, selected, axis=2).astype(jnp.float32) - complex_dot(hidden, jnp.take(iface_cols, selected, axis=2))
    return merged.astype(jnp.bfloat16)


def reference(leaf_maps, w_first, w_second, skel_first, skel_second):
    outputs = []
    for tree_index in range(TREES):
        leaves = leaf_maps[:, tree_index].reshape(2, PARENTS, 2, 3 * K, 3 * K)
        w_one = w_first[:, tree_index].reshape(2, PARENTS, K, K)
        w_two = w_second[:, tree_index].reshape(2, GRANDS, K, K)

        def level_one(parent):
            return merge_pair(leaves[:, parent, 0], leaves[:, parent, 1], w_one[:, parent],
                              skel_first[tree_index, parent], True)

        parents = lax.map(level_one, jnp.arange(PARENTS).astype(jnp.int32))
        paired = parents.reshape(GRANDS, 2, 2, 3 * K, 3 * K)

        def level_two(grand_index):
            return merge_pair(paired[grand_index, 0], paired[grand_index, 1], w_two[:, grand_index],
                              skel_second[tree_index, grand_index], False)

        grands = lax.map(level_two, jnp.arange(GRANDS).astype(jnp.int32))
        outputs.append(jnp.transpose(grands, (1, 0, 2, 3)).reshape(2, GRANDS * 4 * K, 3 * K))
    return jnp.stack(outputs, axis=1)
```

```python
import functools

import jax
import jax.numpy as jnp
from jax import lax
from jax.experimental import pallas as pl
from jax.experimental.pallas import tpu as pltpu
from jax.sharding import PartitionSpec as P

K = 512
BF = jnp.bfloat16
F32 = jnp.float32
MESH = pl.DeviceIdType.MESH


def fdot(a, b):
    return jnp.dot(a, b, preferred_element_type=F32)


def remote(src, dst, send, recv, target):
    return pltpu.make_async_remote_copy(
        src_ref=src, dst_ref=dst, send_sem=send, recv_sem=recv, device_id=target, device_id_type=MESH
    )


def write_left(ref, real, imag):
    n = real.shape[0]
    ref[0:n, 0:K] = real
    ref[0:n, K : 2 * K] = -imag
    ref[n : 2 * n, 0:K] = imag
    ref[n : 2 * n, K : 2 * K] = real


class Spread:
    def __init__(self, buf, send, recv, dsend, drecv, b, f, c, fr):
        self.buf, self.send, self.recv, self.dsend, self.drecv = buf, send, recv, dsend, drecv
        self.c, self.fr, self.b = c, fr, b
        y, xh = f // 2, f % 2
        self.own = f
        self.up = ((y + 1) % 4) * 2 + xh
        self.down = ((y + 3) % 4) * 2 + xh
        self.far = ((y + 2) % 4) * 2 + xh
        self.side = y * 2 + (1 - xh)
        self.up_side = ((y + 1) % 4) * 2 + (1 - xh)
        self.down_side = ((y + 3) % 4) * 2 + (1 - xh)
        self.far_side = ((y + 2) % 4) * 2 + (1 - xh)
        half = fr // 2
        self.c0 = {
            0: (self.own, 0, self.up),
            1: (self.own, 1, self.down),
            2: (self.own, 0, self.side),
            3: (self.own, 1, self.up),
            4: (self.own, 0, self.down),
            5: (self.own, 1, self.side),
            6: (self.down, 0, self.up),
            7: (self.up, 1, self.down),
            8: (self.side, 0, self.up),
            9: (self.side, 0, self.down),
            10: (self.side, 1, self.up),
            11: (self.side, 1, self.down),
            12: (self.far, 0, self.side),
            13: (self.far, 1, self.side),
        }
        self.d0 = [
            (self.own, 0, fr),
            (self.down, 0, fr),
            (self.up, 0, fr),
            (self.side, 0, fr),
            (self.far, 0, half),
            (self.far, half, half),
            (self.down_side, 0, fr),
            (self.up_side, 0, fr),
            (self.far_side, 0, half),
            (self.far_side, half, half),
        ]

    def rows(self, face, at, n):
        return self.buf.at[pl.ds(pl.multiple_of(self.c * K + face * self.fr + at, 16), n), :]

    def hop(self, k):
        face, half, to = self.c0[k]
        view = self.rows(face, half * (self.fr // 2), self.fr // 2)
        return remote(view, view, self.send.at[k], self.recv.at[k], (self.b, to))

    def over(self, k):
        face, at, n = self.d0[k]
        view = self.rows(face, at, n)
        return remote(view, view, self.dsend.at[k], self.drecv.at[k], (self.b + 1 - 2 * self.c, self.own))

    def got(self, *ks):
        for k in ks:
            self.hop(k).wait_recv()

    def go(self, *ks):
        for k in ks:
            self.hop(k).start()

    def hand(self, *ks):
        for k in ks:
            self.over(k).start()

    def begin(self):
        self.go(0, 1, 2, 3, 4, 5)
        self.hand(0)

    def first(self):
        self.got(0)
        self.go(6)
        self.got(1)
        self.go(7)
        self.got(2)
        self.go(8, 9)
        self.got(3)
        self.hand(1)
        self.got(4)
        self.hand(2)
        self.got(5)
        self.go(10, 11)
        self.hand(3)

    def second(self):
        self.got(6)
        self.go(12)
        self.hand(4)
        self.got(7)
        self.go(13)
        self.hand(5)

    def third(self):
        self.got(8, 10)
        self.hand(6)
        self.got(9, 11)
        self.hand(7)
        self.got(12)
        self.hand(8)
        self.got(13)
        self.hand(9)

    def finish(self):
        for k in range(10):
            self.over(k).wait_recv()

    def drain(self):
        for k in range(14):
            self.hop(k).wait_send()
        for k in range(10):
            self.over(k).wait_send()


def kernel(fr, leaf, w1, w2, skel1, skel2, out, ifc, endr, xs, sel, srow, p1, p2, skt, wa, wb, ga, gb,
           lh, lh2, lhs_s, lh2_s, dp, dps, eb, r2, stg, ex, lsem, ssem, rsem, s1, r1, ds1, dr1, s2, r2s, ds2, dr2,
           asend, arecv, bsend, brecv):
    b, f = lax.axis_index("box"), lax.axis_index("face")
    c, h = b % 2, (b // 2) % 2
    q = b % 4
    sib = (b + 1 - 2 * c, f)
    inner_box = b + 2 - 4 * h
    inner, outer = (inner_box, f), (inner_box, f // 2 * 2 + 1 - f % 2)
    cross = (inner_box + 1 - 2 * c, f)
    mid = c != h

    barrier = pltpu.get_barrier_semaphore()
    peers = [(b, f ^ d) for d in range(1, 8)] + [(sib[0], f ^ d) for d in range(8)] + [inner, outer, cross]
    for peer in peers:
        pl.semaphore_signal(barrier, inc=1, device_id=peer, device_id_type=MESH)

    def local(k, src, dst):
        copy = pltpu.make_async_copy(src, dst, lsem.at[k])
        copy.start()
        return copy

    lw = 3 * 2 * K // 8
    loc_if = local(0, leaf.at[c, 0, 0, 1 - c], ifc.at[c])
    loc_end = local(1, leaf.at[:, 0, 0, c], endr)
    own_rows = pl.ds(pl.multiple_of(c * K + f * fr, 16), fr)

    def chunk_of(j):
        return leaf.at[j // 4, 0, 0, 2, :, pl.ds(pl.multiple_of(lw * (j % 4), 128), lw)]

    loc_xs = local(2, chunk_of(f), xs.at[own_rows, :])
    w1_rows = pl.ds(pl.multiple_of(c * (K // 2), 16), K // 2)
    w2_rows = pl.ds(pl.multiple_of(q * (K // 4), 16), K // 4)
    loc_w1 = local(3, w1.at[:, 0], wa.at[:, w1_rows, :])
    loc_w2 = local(4, w2.at[:, 0], wb.at[:, w2_rows, :])

    sk1 = skel1[0, pl.ds(b // 2, 1), :]
    sk2 = skel2[0, pl.ds(b // 4, 1), :]
    for part in range(4):
        at = part * 256
        index = lax.broadcasted_iota(jnp.int32, (256, K), 0) + at
        p1[at : at + 256, :] = jnp.where(index == sk1, 1.0, 0.0).astype(BF)
        p2[at : at + 256, :] = jnp.where(index == sk2, 1.0, 0.0).astype(BF)
    skt[...] = jnp.transpose(jnp.broadcast_to(sk1.astype(F32), (128, K)))

    pl.semaphore_wait(barrier, len(peers))

    t_if = remote(leaf.at[1 - c, 0, 0, 1 - c], ifc.at[c], ssem.at[0], rsem.at[0], sib)
    t_w1 = remote(w1.at[:, 0], wa.at[:, w1_rows, :], ssem.at[1], rsem.at[1], sib)
    t_w2 = remote(w2.at[:, 0], wb.at[:, w2_rows, :], ssem.at[2], rsem.at[2], sib)
    t_w2i = remote(w2.at[0, 0], wb.at[0, w2_rows, :], ssem.at[3], rsem.at[3], inner)
    t_w2o = remote(w2.at[1, 0], wb.at[1, w2_rows, :], ssem.at[4], rsem.at[4], outer)
    q2 = pl.ds(pl.multiple_of((q + 2 - 4 * h) * (K // 4), 16), K // 4)
    t_w2fi = remote(wb.at[0, q2, :], wb.at[0, q2, :], ssem.at[5], rsem.at[5], sib)
    t_w2fo = remote(wb.at[1, q2, :], wb.at[1, q2, :], ssem.at[6], rsem.at[6], sib)
    own_xs = pl.ds(pl.multiple_of(c * K, 16), K)
    t_xs = remote(xs.at[own_xs, :], xs.at[own_xs, :], ssem.at[7], rsem.at[7], sib)

    t_if.start()
    first_a = []
    for d in (7, 6, 5, 4, 3, 2, 1):
        copy = remote(chunk_of(f ^ d), xs.at[own_rows, :], asend.at[d - 1], arecv.at[d - 1], (b, f ^ d))
        copy.start()
        first_a.append(copy)
    t_w1.start()
    t_w2.start()

    ag1 = Spread(ga, s1, r1, ds1, dr1, b, f, c, fr)
    ag2 = Spread(gb, s2, r2s, ds2, dr2, b, f, c, fr)

    loc_if.wait()
    t_if.wait_recv()
    ga[own_rows, 0:K] = ifc[0, :, 0:K]
    ga[own_rows, K : 2 * K] = ifc[1, :, K : 2 * K]
    ga[own_rows, 2 * K :] = (
        fdot(ifc[0, :, 2 * K :], p1[0:K, :]) + fdot(ifc[1, :, 2 * K :], p1[K:, :])
    ).astype(BF)
    ag1.begin()

    def coupled(rows, side, left, left2, weights, pick, dest):
        couple = rows[:, :, pl.ds(pl.multiple_of((1 - side) * K, 128), K)]
        write_left(left, couple[0], couple[1])
        hid = fdot(left[...], weights[...].reshape(2 * K, K)).astype(BF)
        write_left(left2, hid[:fr], hid[fr:])
        side_cols = rows[:, :, 2 * K :].reshape(2 * fr, K)
        half = pick[pl.ds(pl.multiple_of(side * K, 16), K), :]
        dest[...] = fdot(side_cols, half).astype(BF)

    def merged(rows, side, left2, gathered, dest, block):
        prod = fdot(left2[...], gathered[:, block * K : (block + 1) * K])
        if block == 2:
            base = dest[...].astype(F32)
        else:
            on = jnp.where(side == block, 1.0, 0.0)
            base = rows[:, :, block * K : (block + 1) * K].reshape(2 * fr, K).astype(F32) * on
        return (base - prod).astype(BF).reshape(2, fr, K)

    loc_end.wait()
    loc_w1.wait()
    t_w1.wait_recv()
    coupled(endr, c, lh, lh2, wa, p1, dp)

    ag1.first()
    t_w2i.start()
    t_w2o.start()
    loc_xs.wait()
    for copy in first_a:
        copy.wait_recv()
    t_xs.start()
    ag1.second()

    t_xs.wait_recv()
    lane = lax.broadcasted_iota(jnp.int32, (256, 128), 1)
    mine = skt[pl.ds(pl.multiple_of(c * 256, 16), 256), :].astype(jnp.int32)
    total = None
    for part in range(8):
        hot = jnp.where(mine == lane + part * 128, 1.0, 0.0).astype(BF)
        term = fdot(hot, xs[part * 128 : (part + 1) * 128, :])
        total = term if total is None else total + term
    sel[...] = total.astype(BF)
    into = srow.at[f // 4, :, pl.ds(pl.multiple_of(lw * (f % 4), 128), lw)]
    dest_box = b - c + 1 - h
    for i in range(4):
        turn = (f + i) % 4
        src = sel.at[pl.ds(pl.multiple_of(turn * fr, 16), fr), :]
        copy = remote(src, into, bsend.at[i], brecv.at[f], (dest_box, 4 * c + turn))
        if i == 0:
            here = jnp.logical_and(f // 4 == c, mid)

            @pl.when(here)
            def _():
                pltpu.make_async_copy(src, into, brecv.at[f]).start()

            @pl.when(jnp.logical_not(here))
            def _():
                copy.start()
        else:
            copy.start()

    ag1.third()
    ag1.finish()

    for block in (2, 0, 1):
        eb[:, :, block * K : (block + 1) * K] = merged(endr, c, lh2, ga, dp, block)

    ex_own = [remote(stg.at[1 - c], ex.at[h], ssem.at[8], rsem.at[8], sib),
              remote(stg.at[1 - c], ex.at[h], ssem.at[9], rsem.at[9], cross),
              remote(stg.at[c], ex.at[h], ssem.at[10], rsem.at[10], inner)]

    @pl.when(mid)
    def _():
        stg[:, :, 0:K] = eb[:, :, pl.ds(pl.multiple_of(h * K, 128), K)]
        half = p2[pl.ds(pl.multiple_of(h * K, 16), K), :]
        stg[:, :, K:] = fdot(eb[:, :, 2 * K :].reshape(2 * fr, K), half).astype(BF).reshape(2, fr, K)
        for copy in ex_own:
            copy.start()
        ex[h] = stg[c]
        ex_own[1].wait_recv()

    @pl.when(jnp.logical_not(mid))
    def _():
        ex_own[0].wait_recv()
        ex_own[2].wait_recv()

    gb[own_rows, 0:K] = ex[0, :, 0:K]
    gb[own_rows, K : 2 * K] = ex[1, :, 0:K]
    gb[own_rows, 2 * K :] = ex[0, :, K:] + ex[1, :, K:]
    ag2.begin()

    @pl.when(mid)
    def _():
        for j in range(8):
            view = srow.at[j // 4, :, lw * (j % 4) : lw * (j % 4 + 1)]
            pltpu.make_async_copy(view, view, brecv.at[j]).wait()
        seen = skt[pl.ds(pl.multiple_of(f * fr, 16), fr), :]
        left1 = jnp.tile(jnp.where(seen < K, 1.0, 0.0), (1, 4)).astype(BF)
        right1 = 1 - left1
        left = jnp.concatenate([left1, left1], axis=0)
        right = 1 - left
        couple = [srow[t, :, K : 2 * K] * left1 + srow[t, :, 0:K] * right1 for t in range(2)]
        write_left(lhs_s, couple[0], couple[1])
        hid = fdot(lhs_s[...], wa[...].reshape(2 * K, K)).astype(BF)
        write_left(lh2_s, hid[:fr], hid[fr:])
        sides = srow[:, :, 2 * K :].reshape(2 * fr, K)
        dps[...] = (fdot(sides * left, p1[0:K, :]) + fdot(sides * right, p1[K:, :])).astype(BF)
        for block in (2, 0, 1):
            prod = fdot(lh2_s[...], ga[:, block * K : (block + 1) * K])
            if block == 2:
                base = dps[...].astype(F32)
            else:
                on = left if block == 0 else right
                base = (srow[:, :, block * K : (block + 1) * K].reshape(2 * fr, K) * on).astype(F32)
            r2[:, :, block * K : (block + 1) * K] = (base - prod).astype(BF).reshape(2, fr, K)

    @pl.when(jnp.logical_not(mid))
    def _():
        r2[...] = eb[...]

    ag2.first()
    t_w2i.wait_recv()
    t_w2fi.start()
    t_w2o.wait_recv()
    t_w2fo.start()
    ag2.second()
    loc_w2.wait()
    t_w2.wait_recv()
    t_w2fi.wait_recv()
    t_w2fo.wait_recv()
    coupled(r2, h, lh, lh2, wb, p2, dp)
    ag2.third()
    ag2.finish()
    for block in (0, 1, 2):
        out[:, 0, :, block * K : (block + 1) * K] = merged(r2, h, lh2, gb, dp, block)

    for copy in [t_if, t_w1, t_w2, t_w2i, t_w2o, t_w2fi, t_w2fo, t_xs] + first_a:
        copy.wait_send()
    for i in range(4):
        turn = (f + i) % 4
        src = sel.at[pl.ds(pl.multiple_of(turn * fr, 16), fr), :]
        copy = remote(src, into, bsend.at[i], brecv.at[f], (dest_box, 4 * c + turn))
        if i == 0:

            @pl.when(jnp.logical_not(here))
            def _():
                copy.wait_send()
        else:
            copy.wait_send()

    @pl.when(mid)
    def _():
        for copy in ex_own:
            copy.wait_send()

    ag1.drain()
    ag2.drain()


def on_device(leaf, w1, w2, skel1, skel2):
    fr = leaf.shape[4]
    any_spec = pl.BlockSpec(memory_space=pl.ANY)
    vmem_spec = pl.BlockSpec(memory_space=pltpu.VMEM)
    dma = pltpu.SemaphoreType.DMA
    lw = 3 * 2 * K // 8
    scratch = [
        pltpu.VMEM((2, fr, 3 * K), BF),
        pltpu.VMEM((2, fr, 3 * K), BF),
        pltpu.VMEM((2 * K, lw), BF),
        pltpu.VMEM((K // 2, lw), BF),
        pltpu.VMEM((2, fr, 3 * K), BF),
        pltpu.VMEM((2 * K, K), BF),
        pltpu.VMEM((2 * K, K), BF),
        pltpu.VMEM((K, 128), F32),
        pltpu.VMEM((2, K, K), BF),
        pltpu.VMEM((2, K, K), BF),
        pltpu.VMEM((2 * K, 3 * K), BF),
        pltpu.VMEM((2 * K, 3 * K), BF),
        pltpu.VMEM((2 * fr, 2 * K), BF),
        pltpu.VMEM((2 * fr, 2 * K), BF),
        pltpu.VMEM((2 * fr, 2 * K), BF),
        pltpu.VMEM((2 * fr, 2 * K), BF),
        pltpu.VMEM((2 * fr, K), BF),
        pltpu.VMEM((2 * fr, K), BF),
        pltpu.VMEM((2, fr, 3 * K), BF),
        pltpu.VMEM((2, fr, 3 * K), BF),
        pltpu.VMEM((2, fr, 2 * K), BF),
        pltpu.VMEM((2, fr, 2 * K), BF),
        dma((5,)),
        dma((11,)),
        dma((11,)),
        dma((14,)),
        dma((14,)),
        dma((10,)),
        dma((10,)),
        dma((14,)),
        dma((14,)),
        dma((10,)),
        dma((10,)),
        dma((7,)),
        dma((7,)),
        dma((4,)),
        dma((8,)),
    ]
    return pl.pallas_call(
        functools.partial(kernel, fr),
        out_shape=jax.ShapeDtypeStruct((2, 1, fr, 3 * K), BF),
        in_specs=[any_spec, any_spec, any_spec, vmem_spec, vmem_spec],
        out_specs=vmem_spec,
        scratch_shapes=scratch,
        compiler_params=pltpu.CompilerParams(
            collective_id=0, has_side_effects=True, vmem_limit_bytes=48 * 1024 * 1024
        ),
    )(leaf, w1, w2, skel1, skel2)


def solution(mesh):
    return jax.shard_map(
        on_device,
        mesh=mesh,
        in_specs=(
            P(None, None, "box", None, "face", None),
            P(None, None, "box", None),
            P(None, None, "box", None),
            P(),
            P(),
        ),
        out_specs=P(None, None, ("box", "face"), None),
        check_vma=False,
    )
```

```python
import functools

import jax
import jax.numpy as jnp
from jax import lax
from jax.experimental import pallas as pl
from jax.experimental.pallas import tpu as pltpu
from jax.sharding import PartitionSpec as P

K = 512
BF = jnp.bfloat16
F32 = jnp.float32
MESH = pl.DeviceIdType.MESH
ROWS_A = 48
EARLY = (3, 5, 7)


def fdot(a, b):
    return jnp.dot(a, b, preferred_element_type=F32)


def remote(src, dst, send, recv, target):
    return pltpu.make_async_remote_copy(
        src_ref=src, dst_ref=dst, send_sem=send, recv_sem=recv, device_id=target, device_id_type=MESH
    )


def write_left(ref, real, imag):
    n = real.shape[0]
    ref[0:n, 0:K] = real
    ref[0:n, K : 2 * K] = -imag
    ref[n : 2 * n, 0:K] = imag
    ref[n : 2 * n, K : 2 * K] = real


class Gather:
    def __init__(self, view, send, recv, dsend, drecv, sib):
        self.view, self.send, self.recv, self.dsend, self.drecv, self.sib = view, send, recv, dsend, drecv, sib
        self.hops, self.hands = [], []

    def hop(self, k):
        what, to = self.hops[k]
        ref = self.view(*what)
        return remote(ref, ref, self.send.at[k], self.recv.at[k], to)

    def hand_over(self, k):
        ref = self.view(*self.hands[k])
        return remote(ref, ref, self.dsend.at[k], self.drecv.at[k], self.sib)

    def got(self, *ks):
        for k in ks:
            self.hop(k).wait_recv()

    def go(self, *ks):
        for k in ks:
            self.hop(k).start()

    def hand(self, *ks):
        for k in ks:
            self.hand_over(k).start()

    def handed(self):
        for k in range(len(self.hands)):
            self.hand_over(k).wait_recv()

    def drain(self):
        for k in range(len(self.hops)):
            self.hop(k).wait_send()
        for k in range(len(self.hands)):
            self.hand_over(k).wait_send()


def face_gather(view, sems, b, f, sib, fr):
    g = Gather(view, *sems, sib)
    y, xh = f // 2, f % 2

    def at(dy, dx):
        return ((y + dy) % 4) * 2 + (xh + dx) % 2

    own, up, down, far = at(0, 0), at(1, 0), at(3, 0), at(2, 0)
    side, up_side, down_side, far_side = at(0, 1), at(1, 1), at(3, 1), at(2, 1)
    first, last, every = (0, ROWS_A), (ROWS_A, fr - ROWS_A), (0, fr)
    lo, hi, full = (0, 3 * K // 2), (3 * K // 2, 3 * K // 2), (0, 3 * K)
    x, u, d = (b, side), (b, up), (b, down)
    g.hops = [
        ((own, first, full), x),
        ((own, last, full), u),
        ((own, last, full), d),
        ((own, first, full), u),
        ((own, first, full), d),
        ((own, last, full), x),
        ((down, last, lo), u),
        ((up, last, hi), d),
        ((down, last, full), x),
        ((up, last, full), x),
        ((side, first, full), u),
        ((side, first, full), d),
        ((far, last, lo), x),
        ((far, last, hi), x),
        ((down, first, lo), u),
        ((up, first, hi), d),
        ((down_side, first, lo), u),
        ((up_side, first, hi), d),
    ]
    g.hands = [
        (own, every, full),
        (side, first, full),
        (down, every, full),
        (up, every, full),
        (far, last, full),
        (far, first, full),
        (side, last, full),
        (down_side, first, full),
        (up_side, first, full),
        (down_side, last, full),
        (up_side, last, full),
        (far_side, last, full),
        (far_side, first, full),
    ]
    return g


def plane_gather(view, sems, b, f, h, cross_box, sib, fr):
    g = Gather(view, *sems, sib)
    y, xh = f // 2, f % 2

    def face(dy, dx):
        return ((y + dy) % 4) * 2 + (xh + dx) % 2

    xs = [(h, 0), (1 - h, 0), (1 - h, 1), (h, 1)]
    ys = [0, 1, 3, 2]

    def node(iy, ix):
        return (xs[ix][0], face(ys[iy], xs[ix][1]))

    alpha, beta, every = (0, fr // 2), (fr // 2, fr // 2), (0, fr)
    lo, hi, full = (0, K // 2), (K // 2, K // 2), (0, K)
    inner, outer = (cross_box, f), (cross_box, face(0, 1))
    up, down = (b, face(1, 0)), (b, face(3, 0))
    g.hops += [
        ((node(0, 0), alpha, full), inner),
        ((node(0, 0), alpha, full), outer),
        ((node(0, 1), alpha, lo), outer),
        ((node(0, 2), alpha, hi), inner),
    ]
    g.hops += [
        ((node(0, 0), beta, full), up),
        ((node(0, 0), beta, full), down),
        ((node(2, 0), beta, lo), up),
        ((node(1, 0), beta, hi), down),
    ]
    for i in range(4):
        g.hops += [
            ((node(0, i), alpha, full), up),
            ((node(0, i), alpha, full), down),
            ((node(2, i), alpha, lo), up),
            ((node(1, i), alpha, hi), down),
        ]
    for i in range(4):
        g.hops += [
            ((node(i, 0), beta, full), inner),
            ((node(i, 0), beta, full), outer),
            ((node(i, 1), beta, lo), outer),
            ((node(i, 2), beta, hi), inner),
        ]
    g.hands = [(node(i // 4, i % 4), every, full) for i in range(16)]
    return g


def kernel(fr, leaf, w1, w2, skel1, skel2, out, sk1v, sk2v, ifc, endr, xs, sel, srow, p1, p2, skt, wa, wb, ga, gt,
           lh, lh2, lhs_s, lh2_s, dp, dps, r2, stg, pex, res, lsem, ssem, rsem, s1, r1, ds1, dr1, s2, r2s, ds2, dr2,
           asend, arecv, bsend, brecv):
    b, f = lax.axis_index("box"), lax.axis_index("face")
    c, h = b % 2, (b // 2) % 2
    q = b % 4
    sib = (b + 1 - 2 * c, f)
    inner_box = b + 2 - 4 * h
    other_face = f // 2 * 2 + 1 - f % 2
    inner, outer = (inner_box, f), (inner_box, other_face)
    cross_box = inner_box + 1 - 2 * c
    mid = c != h

    barrier = pltpu.get_barrier_semaphore()
    peers = [(b, f ^ d) for d in range(1, 8)] + [(sib[0], f ^ d) for d in range(8)]
    peers += [inner, outer, (cross_box, f), (cross_box, other_face)]
    for peer in peers:
        pl.semaphore_signal(barrier, inc=1, device_id=peer, device_id_type=MESH)

    def local(k, src, dst):
        copy = pltpu.make_async_copy(src, dst, lsem.at[k])
        copy.start()
        return copy

    loc_s1 = local(5, skel1, sk1v)
    loc_s2 = local(6, skel2, sk2v)
    lw = 3 * 2 * K // 8
    loc_if = local(0, leaf.at[c, 0, 0, 1 - c], ifc.at[c])
    loc_end = local(1, leaf.at[:, 0, 0, c], endr)
    own_rows = pl.ds(pl.multiple_of(c * K + f * fr, 16), fr)
    face_rows = pl.ds(pl.multiple_of(f * fr, 16), fr)

    def chunk_of(j):
        return leaf.at[j // 4, 0, 0, 2, :, pl.ds(pl.multiple_of(lw * (j % 4), 128), lw)]

    loc_xs = local(2, chunk_of(f), xs.at[own_rows, :])
    w1_rows = pl.ds(pl.multiple_of(c * (K // 2), 16), K // 2)
    w2_rows = pl.ds(pl.multiple_of(q * (K // 4), 16), K // 4)
    loc_w1 = local(3, w1.at[:, 0], wa.at[:, w1_rows, :])
    loc_w2 = local(4, w2.at[:, 0], wb.at[:, w2_rows, :])

    loc_s1.wait()
    loc_s2.wait()
    sk1 = sk1v[0, pl.ds(b // 2, 1), :]
    sk2 = sk2v[0, pl.ds(b // 4, 1), :]
    for part in range(4):
        at = part * 256
        index = lax.broadcasted_iota(jnp.int32, (256, K), 0) + at
        p1[at : at + 256, :] = jnp.where(index == sk1, 1.0, 0.0).astype(BF)
        p2[at : at + 256, :] = jnp.where(index == sk2, 1.0, 0.0).astype(BF)
    skt[...] = jnp.transpose(jnp.broadcast_to(sk1.astype(F32), (128, K)))

    pl.semaphore_wait(barrier, len(peers))

    t_if = remote(leaf.at[1 - c, 0, 0, 1 - c], ifc.at[c], ssem.at[0], rsem.at[0], sib)
    t_w1 = remote(w1.at[:, 0], wa.at[:, w1_rows, :], ssem.at[1], rsem.at[1], sib)
    t_w2 = remote(w2.at[:, 0], wb.at[:, w2_rows, :], ssem.at[2], rsem.at[2], sib)
    t_w2i = remote(w2.at[0, 0], wb.at[0, w2_rows, :], ssem.at[3], rsem.at[3], inner)
    t_w2o = remote(w2.at[1, 0], wb.at[1, w2_rows, :], ssem.at[4], rsem.at[4], outer)
    q2 = pl.ds(pl.multiple_of((q + 2 - 4 * h) * (K // 4), 16), K // 4)
    t_w2fi = remote(wb.at[0, q2, :], wb.at[0, q2, :], ssem.at[5], rsem.at[5], sib)
    t_w2fo = remote(wb.at[1, q2, :], wb.at[1, q2, :], ssem.at[6], rsem.at[6], sib)
    own_xs = pl.ds(pl.multiple_of(c * K, 16), K)
    t_xs = remote(xs.at[own_xs, :], xs.at[own_xs, :], ssem.at[7], rsem.at[7], sib)
    t_pick = remote(stg.at[1 - h], pex, ssem.at[8], rsem.at[8], (cross_box, f))
    first_a = {
        d: remote(chunk_of(f ^ d), xs.at[own_rows, :], asend.at[d - 1], arecv.at[d - 1], (b, f ^ d)) for d in range(1, 8)
    }

    def part_rows(face, rows, cols):
        at, n = rows
        return ga.at[pl.ds(pl.multiple_of(c * K + face * fr + at, 16), n), cols[0] : cols[0] + cols[1]]

    def plane_rows(node, rows, cols):
        at, n = rows
        return gt.at[node[0], :, pl.ds(pl.multiple_of(node[1] * fr + at, 16), n), cols[0] : cols[0] + cols[1]]

    ag1 = face_gather(part_rows, (s1, r1, ds1, dr1), b, f, sib, fr)
    ag2 = plane_gather(plane_rows, (s2, r2s, ds2, dr2), b, f, h, cross_box, sib, fr)

    t_if.start()
    for d in EARLY:
        first_a[d].start()
    t_w1.start()
    t_w2.start()

    loc_if.wait()
    t_if.wait_recv()
    ga[own_rows, 0:K] = ifc[0, :, 0:K]
    ga[own_rows, K : 2 * K] = ifc[1, :, K : 2 * K]
    ga[own_rows, 2 * K :] = (
        fdot(ifc[0, :, 2 * K :], p1[0:K, :]) + fdot(ifc[1, :, 2 * K :], p1[K:, :])
    ).astype(BF)
    ag1.go(0, 1, 2, 3, 4, 5)
    ag1.hand(0)

    def coupled(rows, side, left, left2, weights, pick, dest):
        couple = rows[:, :, pl.ds(pl.multiple_of((1 - side) * K, 128), K)]
        write_left(left, couple[0], couple[1])
        hid = fdot(left[...], weights[...].reshape(2 * K, K)).astype(BF)
        write_left(left2, hid[:fr], hid[fr:])
        side_cols = rows[:, :, 2 * K :].reshape(2 * fr, K)
        half = pick[pl.ds(pl.multiple_of(side * K, 16), K), :]
        dest[...] = fdot(side_cols, half).astype(BF)

    def base_of(rows, side, dest, block):
        if block == 2:
            return dest[...].astype(F32)
        on = jnp.where(side == block, 1.0, 0.0)
        return rows[:, :, block * K : (block + 1) * K].reshape(2 * fr, K).astype(F32) * on

    loc_end.wait()
    loc_w1.wait()
    t_w1.wait_recv()
    coupled(endr, c, lh, lh2, wa, p1, dp)

    ag1.got(1)
    ag1.go(6, 8)
    ag1.got(2)
    ag1.go(7, 9)
    ag1.got(0)
    ag1.go(10, 11)
    ag1.hand(1)
    ag1.got(3)
    ag1.hand(2)
    ag1.got(4)
    ag1.hand(3)
    ag1.go(14, 15)
    ag1.got(6)
    ag1.go(12)
    ag1.got(7)
    ag1.go(13)
    ag1.hand(4)
    for d in range(1, 8):
        if d not in EARLY:
            first_a[d].start()
    ag1.got(5)
    ag1.hand(6)
    ag1.got(8)
    ag1.hand(9)
    ag1.got(9)
    ag1.hand(10)
    ag1.got(10)
    ag1.go(16)
    ag1.hand(7)
    ag1.got(11)
    ag1.go(17)
    ag1.hand(8)
    t_w2i.start()
    t_w2o.start()
    ag1.got(14, 15)
    ag1.hand(5)
    ag1.got(12, 13)
    ag1.hand(11)
    loc_xs.wait()
    for copy in first_a.values():
        copy.wait_recv()
    t_xs.start()
    ag1.got(16, 17)
    ag1.hand(12)
    ag1.handed()

    @pl.when(mid)
    def _():
        sides = (base_of(endr, c, dp, 2) - fdot(lh2[...], ga[:, 2 * K :])).astype(BF)
        half = p2[pl.ds(pl.multiple_of(h * K, 16), K), :]
        stg[...] = fdot(sides, half).astype(BF).reshape(2, fr, K)
        t_pick.start()
        ends = fdot(lh2[...], ga[:, pl.ds(pl.multiple_of(h * K, 128), K)])
        gt[h, 0:2, face_rows, :] = (-ends).astype(BF).reshape(2, fr, K)

    @pl.when(jnp.logical_not(mid))
    def _():
        for block in (2, 0, 1):
            cols = slice(block * K, (block + 1) * K)
            value = base_of(endr, c, dp, block) - fdot(lh2[...], ga[:, cols])
            r2[:, :, cols] = value.astype(BF).reshape(2, fr, K)

    t_xs.wait_recv()
    lane = lax.broadcasted_iota(jnp.int32, (256, 128), 1)
    mine = skt[pl.ds(pl.multiple_of(c * 256, 16), 256), :].astype(jnp.int32)
    total = None
    for part in range(8):
        hot = jnp.where(mine == lane + part * 128, 1.0, 0.0).astype(BF)
        term = fdot(hot, xs[part * 128 : (part + 1) * 128, :])
        total = term if total is None else total + term
    sel[...] = total.astype(BF)
    into = srow.at[f // 4, :, pl.ds(pl.multiple_of(lw * (f % 4), 128), lw)]
    dest_box = b - c + 1 - h
    here = jnp.logical_and(f // 4 == c, mid)

    def back(i):
        turn = (f + i) % 4
        src = sel.at[pl.ds(pl.multiple_of(turn * fr, 16), fr), :]
        return src, remote(src, into, bsend.at[i], brecv.at[f], (dest_box, 4 * c + turn))

    for i in (2, 1, 3):
        back(i)[1].start()

    @pl.when(here)
    def _():
        pltpu.make_async_copy(back(0)[0], into, brecv.at[f]).start()

    @pl.when(jnp.logical_not(here))
    def _():
        back(0)[1].start()

    @pl.when(mid)
    def _():
        t_pick.wait_recv()
        gt[h, 2, face_rows, :] = stg[h] + pex[...]
        ag2.go(0, 1, 4, 5, 24, 25, 8, 9)
        ag2.hand(0)

        for j in range(8):
            view = srow.at[j // 4, :, lw * (j % 4) : lw * (j % 4 + 1)]
            pltpu.make_async_copy(view, view, brecv.at[j]).wait()
        seen = skt[face_rows, :]
        left1 = jnp.tile(jnp.where(seen < K, 1.0, 0.0), (1, 4)).astype(BF)
        right1 = 1 - left1
        left = jnp.concatenate([left1, left1], axis=0)
        right = 1 - left
        couple = [srow[t, :, K : 2 * K] * left1 + srow[t, :, 0:K] * right1 for t in range(2)]
        write_left(lhs_s, couple[0], couple[1])
        hid = fdot(lhs_s[...], wa[...].reshape(2 * K, K)).astype(BF)
        write_left(lh2_s, hid[:fr], hid[fr:])
        sides = srow[:, :, 2 * K :].reshape(2 * fr, K)
        dps[...] = (fdot(sides * left, p1[0:K, :]) + fdot(sides * right, p1[K:, :])).astype(BF)
        for block in (2, 0, 1):
            prod = fdot(lh2_s[...], ga[:, block * K : (block + 1) * K])
            if block == 2:
                base = dps[...].astype(F32)
            else:
                on = left if block == 0 else right
                base = (srow[:, :, block * K : (block + 1) * K].reshape(2 * fr, K) * on).astype(F32)
            r2[:, :, block * K : (block + 1) * K] = (base - prod).astype(BF).reshape(2, fr, K)

        ag2.got(0)
        ag2.go(2)
        ag2.got(1)
        ag2.go(3)
        ag2.got(4)
        ag2.go(6)
        ag2.got(5)
        ag2.go(7)
        ag2.go(12, 13, 28, 29, 16, 17, 32, 33)

    t_w2i.wait_recv()
    t_w2fi.start()
    t_w2o.wait_recv()
    t_w2fo.start()

    @pl.when(mid)
    def _():
        ag2.got(24, 25)
        ag2.go(26, 27)
        ag2.got(8, 9)
        ag2.go(10, 11)
        ag2.got(2, 3)
        ag2.go(20, 21)
        ag2.got(6, 7)
        ag2.go(36, 37)

    loc_w2.wait()
    t_w2.wait_recv()
    t_w2fi.wait_recv()
    t_w2fo.wait_recv()
    coupled(r2, h, lh, lh2, wb, p2, dp)

    @pl.when(mid)
    def _():
        for i in (1, 2, 3):
            ag2.got(8 + 4 * i)
            ag2.go(10 + 4 * i)
            ag2.got(9 + 4 * i)
            ag2.go(11 + 4 * i)
            ag2.got(24 + 4 * i)
            ag2.go(26 + 4 * i)
            ag2.got(25 + 4 * i)
            ag2.go(27 + 4 * i)
            if i == 1:
                ag2.hand(1, 2, 4, 8)
                ag2.got(26, 27)
                ag2.hand(3)
                ag2.got(10, 11)
                ag2.hand(12)
            if i == 2:
                ag2.hand(5, 6, 9, 10)
        for i in (1, 2):
            ag2.got(10 + 4 * i, 11 + 4 * i)
            ag2.got(26 + 4 * i, 27 + 4 * i)
        ag2.hand(13, 14, 7, 11)
        ag2.got(22, 23)
        ag2.got(38, 39)
        ag2.hand(15)

    @pl.when(jnp.logical_not(mid))
    def _():
        ag2.handed()

    left = lh2[...]
    for block in (0, 1, 2):
        cols = slice(block * K, (block + 1) * K)
        if block == 2:
            prod = fdot(left[:, :K], gt[0, 2]) + fdot(left[:, K:], gt[1, 2])
        else:
            prod = fdot(left, gt[block, 0:2].reshape(2 * K, K))
        value = base_of(r2, h, dp, block) - prod
        res[:, 0, :, cols] = value.astype(BF).reshape(2, fr, K)
        view = (slice(None), slice(None), slice(None), cols)
        local(7 + block, res.at[view], out.at[view])

    for copy in [t_if, t_w1, t_w2, t_w2i, t_w2o, t_w2fi, t_w2fo, t_xs] + list(first_a.values()):
        copy.wait_send()
    for i in (1, 2, 3):
        back(i)[1].wait_send()

    @pl.when(jnp.logical_not(here))
    def _():
        back(0)[1].wait_send()

    ag1.drain()

    @pl.when(mid)
    def _():
        t_pick.wait_send()
        ag2.drain()

    for block in range(3):
        view = (slice(None), slice(None), slice(None), slice(block * K, (block + 1) * K))
        pltpu.make_async_copy(res.at[view], out.at[view], lsem.at[7 + block]).wait()


def on_device(leaf, w1, w2, skel1, skel2):
    fr = leaf.shape[4]
    any_spec = pl.BlockSpec(memory_space=pl.ANY)
    dma = pltpu.SemaphoreType.DMA
    lw = 3 * 2 * K // 8
    scratch = [
        pltpu.VMEM(skel1.shape, jnp.int32),
        pltpu.VMEM(skel2.shape, jnp.int32),
        pltpu.VMEM((2, fr, 3 * K), BF),
        pltpu.VMEM((2, fr, 3 * K), BF),
        pltpu.VMEM((2 * K, lw), BF),
        pltpu.VMEM((K // 2, lw), BF),
        pltpu.VMEM((2, fr, 3 * K), BF),
        pltpu.VMEM((2 * K, K), BF),
        pltpu.VMEM((2 * K, K), BF),
        pltpu.VMEM((K, 128), F32),
        pltpu.VMEM((2, K, K), BF),
        pltpu.VMEM((2, K, K), BF),
        pltpu.VMEM((2 * K, 3 * K), BF),
        pltpu.VMEM((2, 3, K, K), BF),
        pltpu.VMEM((2 * fr, 2 * K), BF),
        pltpu.VMEM((2 * fr, 2 * K), BF),
        pltpu.VMEM((2 * fr, 2 * K), BF),
        pltpu.VMEM((2 * fr, 2 * K), BF),
        pltpu.VMEM((2 * fr, K), BF),
        pltpu.VMEM((2 * fr, K), BF),
        pltpu.VMEM((2, fr, 3 * K), BF),
        pltpu.VMEM((2, fr, K), BF),
        pltpu.VMEM((fr, K), BF),
        pltpu.VMEM((2, 1, fr, 3 * K), BF),
        dma((10,)),
        dma((9,)),
        dma((9,)),
        dma((18,)),
        dma((18,)),
        dma((13,)),
        dma((13,)),
        dma((40,)),
        dma((40,)),
        dma((16,)),
        dma((16,)),
        dma((7,)),
        dma((7,)),
        dma((4,)),
        dma((8,)),
    ]
    return pl.pallas_call(
        functools.partial(kernel, fr),
        out_shape=jax.ShapeDtypeStruct((2, 1, fr, 3 * K), BF),
        in_specs=[any_spec] * 5,
        out_specs=any_spec,
        scratch_shapes=scratch,
        compiler_params=pltpu.CompilerParams(
            collective_id=0, has_side_effects=True, vmem_limit_bytes=67043328
        ),
    )(leaf, w1, w2, skel1, skel2)


def solution(mesh):
    return jax.shard_map(
        on_device,
        mesh=mesh,
        in_specs=(
            P(None, None, "box", None, "face", None),
            P(None, None, "box", None),
            P(None, None, "box", None),
            P(),
            P(),
        ),
        out_specs=P(None, None, ("box", "face"), None),
        check_vma=False,
    )
```

```python
import functools

import jax
import jax.numpy as jnp
from jax import lax
from jax.experimental import pallas as pl
from jax.experimental.pallas import tpu as pltpu
from jax.sharding import PartitionSpec as P

K = 512
BF = jnp.bfloat16
F32 = jnp.float32
MESH = pl.DeviceIdType.MESH
GRANT = 48 * 1024 * 1024


def fdot(a, b):
    return jnp.dot(a, b, preferred_element_type=F32)


def remote(src, dst, send, recv, target):
    return pltpu.make_async_remote_copy(
        src_ref=src, dst_ref=dst, send_sem=send, recv_sem=recv, device_id=target, device_id_type=MESH
    )


def write_left(ref, real, imag):
    n = real.shape[0]
    ref[0:n, 0:K] = real
    ref[0:n, K : 2 * K] = -imag
    ref[n : 2 * n, 0:K] = imag
    ref[n : 2 * n, K : 2 * K] = real


class Gather:
    def __init__(self, view, send, recv, dsend, drecv, sib):
        self.view, self.send, self.recv, self.dsend, self.drecv, self.sib = view, send, recv, dsend, drecv, sib
        self.hops, self.hands = [], []

    def hop(self, k):
        what, to = self.hops[k]
        ref = self.view(*what)
        return remote(ref, ref, self.send.at[0], self.recv.at[k], to)

    def hand_over(self, k):
        ref = self.view(*self.hands[k])
        return remote(ref, ref, self.dsend.at[0], self.drecv.at[0], self.sib)

    def got(self, *ks):
        for k in ks:
            self.hop(k).wait_recv()

    def go(self, *ks):
        for k in ks:
            self.hop(k).start()

    def hand(self, *ks):
        for k in ks:
            self.hand_over(k).start()


def settle(view, sem):
    pltpu.make_async_copy(view, view, sem).wait()


def face_gather(view, sems, b, f, c, sib):
    g = Gather(view, *sems, sib)
    y, xh = f // 2, f % 2

    def at(dy, dx):
        return (c, ((y + dy) % 4) * 2 + (xh + dx) % 2)

    own, up, down, far = at(0, 0), at(1, 0), at(3, 0), at(2, 0)
    side, up_side, down_side, far_side = at(0, 1), at(1, 1), at(3, 1), at(2, 1)
    lo, hi, full = (0, K // 2), (K // 2, K // 2), (0, K)
    x, u, d = (b, side[1]), (b, up[1]), (b, down[1])
    for piece in ((0, 1), (2, 1)):
        g.hops += [
            ((own, piece, full), x),
            ((own, piece, full), u),
            ((own, piece, full), d),
            ((side, piece, full), u),
            ((side, piece, full), d),
            ((down, piece, lo), u),
            ((up, piece, hi), d),
            ((down_side, piece, lo), u),
            ((up_side, piece, hi), d),
        ]
    piece = (1, 1)
    g.hops += [
        ((own, piece, full), u),
        ((own, piece, full), d),
        ((own, piece, full), x),
        ((down, piece, lo), u),
        ((up, piece, hi), d),
        ((down, piece, full), x),
        ((up, piece, full), x),
        ((far, piece, lo), x),
        ((far, piece, hi), x),
    ]
    ends, picked, every = (0, 2), (2, 1), (0, 3)
    g.hands = [
        (own, every, full),
        (side, ends, full),
        (down, every, full),
        (up, every, full),
        (side, picked, full),
        (down_side, every, full),
        (up_side, every, full),
        (far, every, full),
        (far_side, ends, full),
        (far_side, picked, full),
    ]
    return g


def plane_gather(view, sems, b, f, h, cross_box, sib, fr):
    g = Gather(view, *sems, sib)
    y, xh = f // 2, f % 2

    def face(dy, dx):
        return ((y + dy) % 4) * 2 + (xh + dx) % 2

    xs = [(h, 0), (1 - h, 0), (1 - h, 1), (h, 1)]
    ys = [0, 1, 3, 2]

    def node(iy, ix):
        return (xs[ix][0], face(ys[iy], xs[ix][1]))

    alpha, beta = (0, fr // 2), (fr // 2, fr // 2)
    lo, hi, full = (0, K // 2), (K // 2, K // 2), (0, K)
    inner, outer = (cross_box, f), (cross_box, face(0, 1))
    up, down = (b, face(1, 0)), (b, face(3, 0))
    g.hops += [
        ((node(0, 0), alpha, full), inner),
        ((node(0, 0), alpha, full), outer),
        ((node(0, 1), alpha, lo), outer),
        ((node(0, 2), alpha, hi), inner),
    ]
    g.hops += [
        ((node(0, 0), beta, full), up),
        ((node(0, 0), beta, full), down),
        ((node(2, 0), beta, lo), up),
        ((node(1, 0), beta, hi), down),
    ]
    for i in range(4):
        g.hops += [
            ((node(0, i), alpha, full), up),
            ((node(0, i), alpha, full), down),
            ((node(2, i), alpha, lo), up),
            ((node(1, i), alpha, hi), down),
        ]
    for i in range(4):
        g.hops += [
            ((node(i, 0), beta, full), inner),
            ((node(i, 0), beta, full), outer),
            ((node(i, 1), beta, lo), outer),
            ((node(i, 2), beta, hi), inner),
        ]
    g.hands = [(node(i // 2 // 4, i // 2 % 4), (alpha, beta)[i % 2], full) for i in range(32)]
    return g


def kernel(fr, leaf, w1, w2, skel1, skel2, out, sk1v, sk2v, ifs, endr, xs, sel, srow, p1, p2, skt, wa, wb, ga, gt,
           lh, lh2, lhs_s, lh2_s, dp, dps, r2, stg, pex, lsem, ssem, rsem, s1, r1, ds1, dr1, s2, r2s, ds2, dr2,
           asend, arecv, bsend, brecv):
    b, f = lax.axis_index("box"), lax.axis_index("face")
    c, h = b % 2, (b // 2) % 2
    q = b % 4
    sib = (b + 1 - 2 * c, f)
    inner_box = b + 2 - 4 * h
    other_face = f // 2 * 2 + 1 - f % 2
    inner, outer = (inner_box, f), (inner_box, other_face)
    cross_box = inner_box + 1 - 2 * c
    mid = c != h
    not_mid = jnp.logical_not(mid)

    barrier = pltpu.get_barrier_semaphore()
    peers = [(b, f ^ d) for d in range(1, 8)] + [(sib[0], f ^ d) for d in range(8)]
    peers += [inner, outer, (cross_box, f), (cross_box, other_face)]
    for peer in peers:
        pl.semaphore_signal(barrier, inc=1, device_id=peer, device_id_type=MESH)

    def local(k, src, dst):
        copy = pltpu.make_async_copy(src, dst, lsem.at[k])
        copy.start()
        return copy

    loc_s1 = local(5, skel1, sk1v)
    loc_s2 = local(6, skel2, sk2v)
    lw = 3 * 2 * K // 8
    face_rows = pl.ds(pl.multiple_of(f * fr, 16), fr)
    own_rows = pl.ds(pl.multiple_of(c * K + f * fr, 16), fr)
    own_cols = pl.ds(pl.multiple_of(c * K, 128), K)
    loc_ga = local(7, leaf.at[:, 0, 0, 1 - c, :, own_cols], ga.at[c, 0:2, face_rows, :])
    loc_if = local(0, leaf.at[c, 0, 0, 1 - c, :, 2 * K : 3 * K], ifs.at[c])
    loc_end = local(1, leaf.at[:, 0, 0, c], endr)

    def chunk_of(j):
        return leaf.at[j // 4, 0, 0, 2, :, pl.ds(pl.multiple_of(lw * (j % 4), 128), lw)]


    @pl.when(not_mid)
    def _():
        pltpu.make_async_copy(chunk_of(f), xs.at[own_rows, :], lsem.at[2]).start()

    w1_rows = pl.ds(pl.multiple_of(c * (K // 2), 16), K // 2)
    w2_rows = pl.ds(pl.multiple_of(q * (K // 4), 16), K // 4)
    loc_w1 = local(3, w1.at[:, 0], wa.at[:, w1_rows, :])
    loc_w2 = local(4, w2.at[:, 0], wb.at[:, w2_rows, :])

    loc_s1.wait()
    loc_s2.wait()
    sk1 = sk1v[0, pl.ds(b // 2, 1), :]
    sk2 = sk2v[0, pl.ds(b // 4, 1), :]
    for part in range(4):
        at = part * 256
        index = lax.broadcasted_iota(jnp.int32, (256, K), 0) + at
        p1[at : at + 256, :] = jnp.where(index == sk1, 1.0, 0.0).astype(BF)
        p2[at : at + 256, :] = jnp.where(index == sk2, 1.0, 0.0).astype(BF)
    skt[...] = jnp.transpose(jnp.broadcast_to(sk1.astype(F32), (128, K)))
    loc_ga.wait()

    pl.semaphore_wait(barrier, len(peers))

    t_if = remote(leaf.at[1 - c, 0, 0, 1 - c, :, 2 * K : 3 * K], ifs.at[c], ssem.at[0], rsem.at[0], sib)
    t_w1 = remote(w1.at[:, 0], wa.at[:, w1_rows, :], ssem.at[1], rsem.at[1], sib)
    t_w2 = remote(w2.at[:, 0], wb.at[:, w2_rows, :], ssem.at[2], rsem.at[2], sib)
    t_w2i = remote(w2.at[0, 0], wb.at[0, w2_rows, :], ssem.at[3], rsem.at[3], inner)
    t_w2o = remote(w2.at[1, 0], wb.at[1, w2_rows, :], ssem.at[4], rsem.at[4], outer)
    q2 = pl.ds(pl.multiple_of((q + 2 - 4 * h) * (K // 4), 16), K // 4)
    t_w2fi = remote(wb.at[0, q2, :], wb.at[0, q2, :], ssem.at[5], rsem.at[5], sib)
    t_w2fo = remote(wb.at[1, q2, :], wb.at[1, q2, :], ssem.at[6], rsem.at[6], sib)
    t_xs = remote(chunk_of(f), xs.at[own_rows, :], ssem.at[7], rsem.at[7], sib)
    t_pick = remote(stg.at[1 - h], pex, ssem.at[8], rsem.at[8], (cross_box, f))
    picker_box = b - c + h

    def spread_side():
        for d in (7, 5, 3, 1, 6, 4, 2):
            remote(chunk_of(f ^ d), xs.at[own_rows, :], asend.at[0], arecv.at[0], (picker_box, f ^ d)).start()


    def part_rows(node, blocks, cols):
        rows = pl.ds(pl.multiple_of(node[1] * fr, 16), fr)
        return ga.at[node[0], blocks[0] : blocks[0] + blocks[1], rows, cols[0] : cols[0] + cols[1]]

    def plane_rows(node, rows, cols):
        at, n = rows
        return gt.at[node[0], :, pl.ds(pl.multiple_of(node[1] * fr + at, 16), n), cols[0] : cols[0] + cols[1]]

    ag1 = face_gather(part_rows, (s1, r1, ds1, dr1), b, f, c, sib)
    ag2 = plane_gather(plane_rows, (s2, r2s, ds2, dr2), b, f, h, cross_box, sib, fr)

    t_if.start()
    ag1.go(18, 19, 0, 1, 2, 20)
    t_w1.start()
    t_w2.start()

    loc_if.wait()
    t_if.wait_recv()
    ga[c, 2, face_rows, :] = (fdot(ifs[0], p1[0:K, :]) + fdot(ifs[1], p1[K:, :])).astype(BF)
    ag1.go(9, 10, 11)
    ag1.hand(0)

    def coupled(rows, side, left, left2, weights, pick, dest):
        couple = rows[:, :, pl.ds(pl.multiple_of((1 - side) * K, 128), K)]
        write_left(left, couple[0], couple[1])
        hid = fdot(left[...], weights[...].reshape(2 * K, K)).astype(BF)
        write_left(left2, hid[:fr], hid[fr:])
        side_cols = rows[:, :, 2 * K :].reshape(2 * fr, K)
        half = pick[pl.ds(pl.multiple_of(side * K, 16), K), :]
        dest[...] = fdot(side_cols, half).astype(BF)

    def base_of(rows, side, dest, block):
        if block == 2:
            return dest[...].astype(F32)
        on = jnp.where(side == block, 1.0, 0.0)
        return rows[:, :, block * K : (block + 1) * K].reshape(2 * fr, K).astype(F32) * on

    def times(left2, gathered, block):
        if block == 2:
            left = left2[...]
            return fdot(left[:, :K], gathered[0, 2]) + fdot(left[:, K:], gathered[1, 2])
        return fdot(left2[...], gathered[block, 0:2].reshape(2 * K, K))

    loc_end.wait()
    loc_w1.wait()
    t_w1.wait_recv()
    coupled(endr, c, lh, lh2, wa, p1, dp)

    ag1.got(18)
    ag1.go(21, 23)
    ag1.got(19)
    ag1.go(22, 24)
    ag1.got(0)
    ag1.go(3, 4)
    ag1.got(1)
    ag1.go(5)
    ag1.got(2)
    ag1.go(6)
    ag1.got(20)
    ag1.hand(1)
    ag1.got(21)
    ag1.go(25)
    ag1.got(22)
    ag1.go(26)
    t_w2i.start()
    t_w2o.start()
    ag1.got(9)
    ag1.go(12, 13)
    ag1.hand(4)
    ag1.got(10)
    ag1.go(14)
    ag1.hand(2)
    ag1.got(11)
    ag1.go(15)
    ag1.hand(3)
    ag1.got(3)
    ag1.go(7)
    ag1.got(4)
    ag1.go(8)
    ag1.got(12)
    ag1.go(16)
    ag1.got(13)
    ag1.go(17)

    @pl.when(mid)
    def _():
        t_xs.start()
        spread_side()

    ag1.got(23)
    ag1.hand(5)
    ag1.got(24)
    ag1.hand(6)
    ag1.got(5, 6, 14, 15)
    ag1.hand(7)
    ag1.got(25, 26, 7, 8)
    ag1.hand(8)
    ag1.got(16, 17)
    ag1.hand(9)

    @pl.when(not_mid)
    def _():
        spread_side()

    settle(ga.at[0], dr1.at[0])

    into = srow.at[f // 4, :, pl.ds(pl.multiple_of(lw * (f % 4), 128), lw)]
    dest_box = b - c + 1 - h

    def pass_w2():
        t_w2i.wait_recv()
        t_w2fi.start()
        t_w2o.wait_recv()
        t_w2fo.start()

    def side_select():
        pltpu.make_async_copy(chunk_of(f), xs.at[own_rows, :], lsem.at[2]).wait()
        t_xs.wait_recv()
        settle(xs.at[0 : 14 * fr, :], arecv.at[0])
        lane = lax.broadcasted_iota(jnp.int32, (K, 128), 1)
        mine = skt[...].astype(jnp.int32)
        total = None
        for part in range(8):
            hot = jnp.where(mine == lane + part * 128, 1.0, 0.0).astype(BF)
            term = fdot(hot, xs[part * 128 : (part + 1) * 128, :])
            total = term if total is None else total + term
        sel[...] = total.astype(BF)
        for d in (7, 5, 3, 1, 6, 4, 2, 0):
            rows = pl.ds(pl.multiple_of((f ^ d) * fr, 16), fr)
            remote(sel.at[rows, :], into, bsend.at[0], brecv.at[0], (dest_box, f ^ d)).start()

    def level_two():
        loc_w2.wait()
        t_w2.wait_recv()
        t_w2fi.wait_recv()
        t_w2fo.wait_recv()
        coupled(r2, h, lh, lh2, wb, p2, dp)

    def third(i):
        ag2.got(8 + 4 * i)
        ag2.go(10 + 4 * i)
        ag2.hand(2 * (8 + i))
        ag2.got(9 + 4 * i)
        ag2.go(11 + 4 * i)
        ag2.hand(2 * (4 + i))
        ag2.got(24 + 4 * i)
        ag2.go(26 + 4 * i)
        ag2.hand(2 * (4 * i + 1) + 1)
        ag2.got(25 + 4 * i)
        ag2.go(27 + 4 * i)
        ag2.hand(2 * (4 * i + 2) + 1)

    @pl.when(mid)
    def _():
        sides = (base_of(endr, c, dp, 2) - times(lh2, ga, 2)).astype(BF)
        half = p2[pl.ds(pl.multiple_of(h * K, 16), K), :]
        stg[...] = fdot(sides, half).astype(BF).reshape(2, fr, K)
        t_pick.start()
        ends = fdot(lh2[...], ga[h, 0:2].reshape(2 * K, K))
        gt[h, 0:2, face_rows, :] = (-ends).astype(BF).reshape(2, fr, K)
        pass_w2()
        t_pick.wait_recv()
        gt[h, 2, face_rows, :] = stg[h] + pex[...]
        ag2.go(0, 1, 4, 5, 24, 25, 8, 9)
        ag2.hand(0, 1)
        ag2.got(0)
        ag2.go(2)
        ag2.got(1)
        ag2.go(3)
        ag2.got(4)
        ag2.go(6)
        ag2.got(5)
        ag2.go(7)
        ag2.go(12, 13, 28, 29, 16, 17, 32, 33)
        ag2.hand(2, 4, 9, 17)
        ag2.got(24, 25)
        ag2.go(26, 27)
        ag2.got(8, 9)
        ag2.go(10, 11)
        ag2.hand(3, 5, 8, 16)
        ag2.got(2, 3)
        ag2.go(20, 21)
        ag2.got(6, 7)
        ag2.go(36, 37)
        ag2.hand(6, 25)
        third(1)
        ag2.got(26, 27)
        ag2.got(10, 11)
        ag2.hand(7, 24)

        settle(srow, brecv.at[0])
        seen = skt[face_rows, :]
        left1 = jnp.tile(jnp.where(seen < K, 1.0, 0.0), (1, 4)).astype(BF)
        right1 = 1 - left1
        left = jnp.concatenate([left1, left1], axis=0)
        right = 1 - left
        couple = [srow[t, :, K : 2 * K] * left1 + srow[t, :, 0:K] * right1 for t in range(2)]
        write_left(lhs_s, couple[0], couple[1])
        hid = fdot(lhs_s[...], wa[...].reshape(2 * K, K)).astype(BF)
        write_left(lh2_s, hid[:fr], hid[fr:])
        sides = srow[:, :, 2 * K :].reshape(2 * fr, K)
        dps[...] = (fdot(sides * left, p1[0:K, :]) + fdot(sides * right, p1[K:, :])).astype(BF)
        for block in (2, 0, 1):
            if block == 2:
                base = dps[...].astype(F32)
            else:
                on = left if block == 0 else right
                base = (srow[:, :, block * K : (block + 1) * K].reshape(2 * fr, K) * on).astype(F32)
            value = base - times(lh2_s, ga, block)
            r2[:, :, block * K : (block + 1) * K] = value.astype(BF).reshape(2, fr, K)

        third(2)
        level_two()
        third(3)
        for i in (1, 2):
            ag2.got(10 + 4 * i, 11 + 4 * i)
            ag2.hand(2 * (12 + i))
            ag2.got(26 + 4 * i, 27 + 4 * i)
            ag2.hand(2 * (4 * i + 3) + 1)
        ag2.got(22, 23)
        ag2.hand(30)
        ag2.got(38, 39)
        ag2.hand(31)

    @pl.when(not_mid)
    def _():
        for block in (2, 0, 1):
            value = base_of(endr, c, dp, block) - times(lh2, ga, block)
            r2[:, :, block * K : (block + 1) * K] = value.astype(BF).reshape(2, fr, K)
        pass_w2()
        side_select()
        level_two()
        settle(gt, dr2.at[0])

    for block in (0, 1, 2):
        value = base_of(r2, h, dp, block) - times(lh2, gt, block)
        out[:, 0, :, block * K : (block + 1) * K] = value.astype(BF).reshape(2, fr, K)

    for copy in [t_if, t_w1, t_w2, t_w2i, t_w2o, t_w2fi, t_w2fo]:
        copy.wait_send()
    settle(xs.at[0 : 7 * fr, :], asend.at[0])
    settle(ga.at[0, :, 0 : 7 * fr, :], s1.at[0])
    settle(ga.at[0], ds1.at[0])

    @pl.when(mid)
    def _():
        t_xs.wait_send()
        t_pick.wait_send()
        settle(gt.at[:, :, 0 : K - fr // 2, :], s2.at[0])
        settle(gt, ds2.at[0])

    @pl.when(not_mid)
    def _():
        settle(sel, bsend.at[0])


def on_device(leaf, w1, w2, skel1, skel2):
    fr = leaf.shape[4]
    hbm_spec = pl.BlockSpec(memory_space=pltpu.HBM)
    dma = pltpu.SemaphoreType.DMA
    lw = 3 * 2 * K // 8
    scratch = [
        pltpu.VMEM(skel1.shape, jnp.int32),
        pltpu.VMEM(skel2.shape, jnp.int32),
        pltpu.VMEM((2, fr, K), BF),
        pltpu.VMEM((2, fr, 3 * K), BF),
        pltpu.VMEM((2 * K, lw), BF),
        pltpu.VMEM((K, lw), BF),
        pltpu.VMEM((2, fr, 3 * K), BF),
        pltpu.VMEM((2 * K, K), BF),
        pltpu.VMEM((2 * K, K), BF),
        pltpu.VMEM((K, 128), F32),
        pltpu.VMEM((2, K, K), BF),
        pltpu.VMEM((2, K, K), BF),
        pltpu.VMEM((2, 3, K, K), BF),
        pltpu.VMEM((2, 3, K, K), BF),
        pltpu.VMEM((2 * fr, 2 * K), BF),
        pltpu.VMEM((2 * fr, 2 * K), BF),
        pltpu.VMEM((2 * fr, 2 * K), BF),
        pltpu.VMEM((2 * fr, 2 * K), BF),
        pltpu.VMEM((2 * fr, K), BF),
        pltpu.VMEM((2 * fr, K), BF),
        pltpu.VMEM((2, fr, 3 * K), BF),
        pltpu.VMEM((2, fr, K), BF),
        pltpu.VMEM((fr, K), BF),
        dma((8,)),
        dma((9,)),
        dma((9,)),
        dma((1,)),
        dma((27,)),
        dma((1,)),
        dma((1,)),
        dma((1,)),
        dma((40,)),
        dma((1,)),
        dma((1,)),
        dma((1,)),
        dma((1,)),
        dma((1,)),
        dma((1,)),
    ]
    return pl.pallas_call(
        functools.partial(kernel, fr),
        out_shape=jax.ShapeDtypeStruct((2, 1, fr, 3 * K), BF),
        in_specs=[hbm_spec] * 5,
        out_specs=pl.BlockSpec(memory_space=pltpu.VMEM),
        scratch_shapes=scratch,
        compiler_params=pltpu.CompilerParams(
            collective_id=0, has_side_effects=True, vmem_limit_bytes=GRANT
        ),
    )(*[pltpu.with_memory_space_constraint(a, pltpu.HBM) for a in (leaf, w1, w2, skel1, skel2)])


def solution(mesh):
    return jax.shard_map(
        on_device,
        mesh=mesh,
        in_specs=(
            P(None, None, "box", None, "face", None),
            P(None, None, "box", None),
            P(None, None, "box", None),
            P(),
            P(),
        ),
        out_specs=P(None, None, ("box", "face"), None),
        check_vma=False,
    )
```

```python
import functools

import jax
import jax.numpy as jnp
from jax import lax
from jax.experimental import pallas as pl
from jax.experimental.pallas import tpu as pltpu
from jax.sharding import PartitionSpec as P

K = 512
BF = jnp.bfloat16
F32 = jnp.float32
MESH = pl.DeviceIdType.MESH
GRANT = 48 * 1024 * 1024


def fdot(a, b):
    return jnp.dot(a, b, preferred_element_type=F32)


def remote(src, dst, send, recv, target):
    return pltpu.make_async_remote_copy(
        src_ref=src, dst_ref=dst, send_sem=send, recv_sem=recv, device_id=target, device_id_type=MESH
    )


def write_left(ref, real, imag):
    n = real.shape[0]
    ref[0:n, 0:K] = real
    ref[0:n, K : 2 * K] = -imag
    ref[n : 2 * n, 0:K] = imag
    ref[n : 2 * n, K : 2 * K] = real


class Gather:
    def __init__(self, view, send, recv, dsend, drecv, sib):
        self.view, self.send, self.recv, self.dsend, self.drecv, self.sib = view, send, recv, dsend, drecv, sib
        self.hops, self.hands, self.split, self.shared = [], [], 8, []

    def hop(self, k):
        what, to = self.hops[k]
        ref = self.view(*what)
        return remote(ref, ref, self.send.at[0], self.recv.at[self.sem_of(k)], to)

    def together(self, slots):
        settle(self.same_bytes(slots, len(slots)), self.recv.at[self.sem_of(slots[0])])

    def hand_over(self, k):
        ref = self.view(*self.hands[k])
        return remote(ref, ref, self.dsend.at[0], self.drecv.at[k // self.split], self.sib)

    def sem_of(self, k):
        first = {slot: group[0] for group in self.shared for slot in group}
        used = [slot for slot in range(len(self.hops)) if first.get(slot, slot) == slot]
        return used.index(first.get(k, k))

    def got(self, *ks):
        for k in ks:
            self.hop(k).wait_recv()

    def go(self, *ks):
        for k in ks:
            self.hop(k).start()

    def hand(self, *ks):
        for k in ks:
            self.hand_over(k).start()


def settle(view, sem):
    pltpu.make_async_copy(view, view, sem).wait()


def face_gather(view, sems, b, f, c, sib):
    g = Gather(view, *sems, sib)
    y, xh = f // 2, f % 2

    def at(dy, dx):
        return (c, ((y + dy) % 4) * 2 + (xh + dx) % 2)

    own, up, down, far = at(0, 0), at(1, 0), at(3, 0), at(2, 0)
    side, up_side, down_side, far_side = at(0, 1), at(1, 1), at(3, 1), at(2, 1)
    lo, hi, full = (0, K // 2), (K // 2, K // 2), (0, K)
    x, u, d = (b, side[1]), (b, up[1]), (b, down[1])
    for piece in ((0, 1), (2, 1)):
        g.hops += [
            ((own, piece, full), x),
            ((own, piece, full), u),
            ((own, piece, full), d),
            ((side, piece, full), u),
            ((side, piece, full), d),
            ((down, piece, lo), u),
            ((up, piece, hi), d),
            ((down_side, piece, lo), u),
            ((up_side, piece, hi), d),
        ]
    piece = (1, 1)
    g.hops += [
        ((own, piece, full), u),
        ((own, piece, full), d),
        ((own, piece, full), x),
        ((down, piece, lo), u),
        ((up, piece, hi), d),
        ((down, piece, full), x),
        ((up, piece, full), x),
        ((far, piece, lo), x),
        ((far, piece, hi), x),
    ]
    ends, picked = (0, 2), (2, 1)
    places = (own, side, down, up, down_side, up_side, far, far_side)
    g.shared = [[5, 6], [7, 8], [14, 15], [16, 17], [25, 26]]
    g.hands = [(place, picked, full) for place in places] + [(place, ends, full) for place in places]
    return g


class Plane(Gather):
    def __init__(self, view, sems, b, f, h, cross_box, sib, fr):
        super().__init__(view, *sems, sib)
        self.split = 32
        y, xh = f // 2, f % 2

        def face(dy, dx):
            return ((y + dy) % 4) * 2 + (xh + dx) % 2

        xs = [(h, 0), (1 - h, 0), (1 - h, 1), (h, 1)]
        ys = [0, 1, 3, 2]

        def node(iy, ix):
            return (xs[ix][0], face(ys[iy], xs[ix][1]))

        lo, hi, full = (0, K // 2), (K // 2, K // 2), (0, K)
        inner, outer = (cross_box, f), (cross_box, face(0, 1))
        up, down = (b, face(1, 0)), (b, face(3, 0))
        for p, piece in enumerate(((0, 0, fr), (1, 0, fr), (2, 0, fr // 2), (2, fr // 2, fr // 2))):

            def line_x():
                return [(own, inner), (own, outer), (own, (b, face(0, 1)))]

            def line_y():
                return [(own, up), (own, down), (own, (b, face(2, 0)))]

            def round_x(iy):
                return [
                    ((node(iy, 0), piece, full), inner),
                    ((node(iy, 0), piece, full), outer),
                    ((node(iy, 1), piece, lo), outer),
                    ((node(iy, 2), piece, hi), inner),
                ]

            def round_y(ix):
                return [
                    ((node(0, ix), piece, full), up),
                    ((node(0, ix), piece, full), down),
                    ((node(2, ix), piece, lo), up),
                    ((node(1, ix), piece, hi), down),
                ]

            own = (node(0, 0), piece, full)
            first, second = (line_x, round_y) if p % 2 == 0 else (line_y, round_x)
            self.hops += first()
            for i in range(4):
                self.hops += second(i)
            self.hands += [(node(i // 4, i % 4), piece, full) for i in range(16)]
            k = 19 * p + 5
            self.shared += [[k, k + 1, k + 4, k + 5, k + 8, k + 9], [k + 12, k + 13]]

    def give(self, p, along, across):
        iy, ix = (across, along) if p % 2 == 0 else (along, across)
        self.hand(16 * p + 4 * iy + ix)

    def start(self, p):
        k = 19 * p
        self.go(k, k + 1, k + 2, k + 3, k + 4)
        self.give(p, 0, 0)

    def near(self, p):
        k = 19 * p
        for slot in (0, 1):
            place = 1 + slot if p % 2 == 0 else 2 - slot
            self.got(k + slot)
            self.go(k + 3 + 4 * place, k + 4 + 4 * place)
            self.give(p, place, 0)

    def two_away(self, p):
        k = 19 * p
        self.got(k + 2)
        self.go(k + 15, k + 16)
        self.give(p, 3, 0)

    def turn(self, p, i):
        k = 19 * p + 3 + 4 * i
        for slot in (0, 1):
            self.got(k + slot)
            self.go(k + 2 + slot)
            self.give(p, i, 2 - slot if p % 2 == 0 else 1 + slot)

    def corners(self, p):
        k = 19 * p + 5
        self.together([k, k + 1, k + 4, k + 5, k + 8, k + 9])
        for i in range(3):
            self.give(p, i, 3)

    def last_corner(self, p):
        k = 19 * p + 17
        self.together([k, k + 1])
        self.give(p, 3, 3)


def kernel(fr, leaf, w1, w2, skel1, skel2, out, sk1v, sk2v, ifs, endr, sraw, xs, sel, srow, p1, p2, skt, wa, wb, ga, gt,
           lh, lh2, lhs_s, lh2_s, dp, dps, r2, stg, pex, lsem, ssem, rsem, s1, r1, ds1, dr1, s2, r2s, ds2, dr2,
           asend, arecv, bsend, brecv):
    b, f = lax.axis_index("box"), lax.axis_index("face")
    c, h = b % 2, (b // 2) % 2
    q = b % 4
    sib = (b + 1 - 2 * c, f)
    inner_box = b + 2 - 4 * h
    other_face = f // 2 * 2 + 1 - f % 2
    inner, outer = (inner_box, f), (inner_box, other_face)
    cross_box = inner_box + 1 - 2 * c
    mid = c != h
    not_mid = jnp.logical_not(mid)

    barrier = pltpu.get_barrier_semaphore()
    up, down = (f + 2) % 8, (f + 6) % 8
    peers = [(b, up), (b, down), (b, other_face), sib, inner, outer, (cross_box, f), (cross_box, other_face)]
    for peer in peers:
        pl.semaphore_signal(barrier, inc=1, device_id=peer, device_id_type=MESH)

    def local(k, src, dst):
        copy = pltpu.make_async_copy(src, dst, lsem.at[k])
        copy.start()
        return copy

    loc_s1 = local(5, skel1, sk1v)
    loc_s2 = local(6, skel2, sk2v)
    lw = 3 * 2 * K // 8
    face_rows = pl.ds(pl.multiple_of(f * fr, 16), fr)
    own_rows = pl.ds(pl.multiple_of(c * K + f * fr, 16), fr)
    own_cols = pl.ds(pl.multiple_of(c * K, 128), K)
    loc_ga = local(7, leaf.at[:, 0, 0, 1 - c, :, own_cols], ga.at[c, 0:2, face_rows, :])
    loc_if = local(0, leaf.at[c, 0, 0, 1 - c, :, 2 * K : 3 * K], ifs.at[c])
    loc_end = local(1, leaf.at[:, 0, 0, c], endr)

    def chunk_of(j):
        return leaf.at[j // 4, 0, 0, 2, :, pl.ds(pl.multiple_of(lw * (j % 4), 128), lw)]


    @pl.when(not_mid)
    def _():
        pltpu.make_async_copy(chunk_of(f), xs.at[own_rows, :], lsem.at[2]).start()

    sib_rows = pl.ds(pl.multiple_of((1 - c) * K + f * fr, 16), fr)

    w1_rows = pl.ds(pl.multiple_of(c * (K // 2), 16), K // 2)
    w2_rows = pl.ds(pl.multiple_of(q * (K // 4), 16), K // 4)
    loc_w1 = local(3, w1.at[:, 0], wa.at[:, w1_rows, :])
    loc_w2 = local(4, w2.at[:, 0], wb.at[:, w2_rows, :])

    loc_ga.wait()

    pl.semaphore_wait(barrier, len(peers))

    t_if = remote(leaf.at[1 - c, 0, 0, 1 - c, :, 2 * K : 3 * K], ifs.at[c], ssem.at[0], rsem.at[0], sib)
    t_w1 = remote(w1.at[:, 0], wa.at[:, w1_rows, :], ssem.at[0], rsem.at[1], sib)
    t_w2 = remote(w2.at[:, 0], wb.at[:, w2_rows, :], ssem.at[0], rsem.at[2], sib)
    t_w2i = remote(w2.at[0, 0], wb.at[0, w2_rows, :], ssem.at[0], rsem.at[3], inner)
    t_w2o = remote(w2.at[1, 0], wb.at[1, w2_rows, :], ssem.at[0], rsem.at[4], outer)
    q2 = pl.ds(pl.multiple_of((q + 2 - 4 * h) * (K // 4), 16), K // 4)
    t_w2fi = remote(wb.at[0, q2, :], wb.at[0, q2, :], ssem.at[0], rsem.at[5], sib)
    t_w2fo = remote(wb.at[1, q2, :], wb.at[1, q2, :], ssem.at[0], rsem.at[6], sib)
    t_side = remote(leaf.at[:, 0, 0, 2], sraw, ssem.at[1], rsem.at[7], sib)
    t_pick = remote(stg.at[1 - h], pex, ssem.at[1], rsem.at[8], (cross_box, f))
    picker_box = b - c + h

    def sib_chunk_of(j):
        return sraw.at[j // 4, :, pl.ds(pl.multiple_of(lw * (j % 4), 128), lw)]

    def spread_side(places, first):
        if first:
            t_side.wait_recv()
            pltpu.make_async_copy(sib_chunk_of(f), xs.at[sib_rows, :], lsem.at[5]).start()
        for d in places:
            to = (picker_box, f ^ d)
            remote(chunk_of(f ^ d), xs.at[own_rows, :], asend.at[0], arecv.at[0], to).start()
            remote(sib_chunk_of(f ^ d), xs.at[sib_rows, :], asend.at[0], arecv.at[0], to).start()

    def part_rows(node, blocks, cols):
        rows = pl.ds(pl.multiple_of(node[1] * fr, 16), fr)
        return ga.at[node[0], blocks[0] : blocks[0] + blocks[1], rows, cols[0] : cols[0] + cols[1]]

    def plane_rows(node, piece, cols):
        block, at, n = piece
        return gt.at[node[0], block, pl.ds(pl.multiple_of(node[1] * fr + at, 16), n), cols[0] : cols[0] + cols[1]]

    def half_ga(slots, n):
        return ga.at[0, 0, 0 : n * fr // 2, :]

    def half_gt(slots, n):
        rows = fr if slots[0] < 38 else fr // 2
        return gt.at[0, 0, 0 : n * rows // 2, :]

    ag1 = face_gather(part_rows, (s1, r1, ds1, dr1), b, f, c, sib)
    ag2 = Plane(plane_rows, (s2, r2s, ds2, dr2), b, f, h, cross_box, sib, fr)
    ag1.same_bytes, ag2.same_bytes = half_ga, half_gt

    t_if.start()
    ag1.go(18, 19, 0)
    ag1.hand(8)
    t_w1.start()
    t_w2.start()

    @pl.when(mid)
    def _():
        t_side.start()


    def one_hot(rows, pick):
        for part in range(4):
            at = part * 256
            index = lax.broadcasted_iota(jnp.int32, (256, K), 0) + at
            pick[at : at + 256, :] = jnp.where(index == rows, 1.0, 0.0).astype(BF)

    loc_s1.wait()
    sk1 = sk1v[0, pl.ds(b // 2, 1), :]
    one_hot(sk1, p1)
    loc_if.wait()
    t_if.wait_recv()
    ga[c, 2, face_rows, :] = (fdot(ifs[0], p1[0:K, :]) + fdot(ifs[1], p1[K:, :])).astype(BF)
    ag1.go(9, 10, 11, 1, 2, 20)
    ag1.hand(0)

    def coupled(rows, side, left, left2, weights, pick, dest):
        couple = rows[:, :, pl.ds(pl.multiple_of((1 - side) * K, 128), K)]
        write_left(left, couple[0], couple[1])
        hid = fdot(left[...], weights[...].reshape(2 * K, K)).astype(BF)
        write_left(left2, hid[:fr], hid[fr:])
        side_cols = rows[:, :, 2 * K :].reshape(2 * fr, K)
        half = pick[pl.ds(pl.multiple_of(side * K, 16), K), :]
        dest[...] = fdot(side_cols, half).astype(BF)

    def base_of(rows, side, dest, block):
        if block == 2:
            return dest[...].astype(F32)
        on = jnp.where(side == block, 1.0, 0.0)
        return rows[:, :, block * K : (block + 1) * K].reshape(2 * fr, K).astype(F32) * on

    def times(left2, gathered, block):
        if block == 2:
            left = left2[...]
            return fdot(left[:, :K], gathered[0, 2]) + fdot(left[:, K:], gathered[1, 2])
        return fdot(left2[...], gathered[block, 0:2].reshape(2 * K, K))

    loc_end.wait()
    loc_w1.wait()
    t_w1.wait_recv()
    coupled(endr, c, lh, lh2, wa, p1, dp)

    skt[...] = jnp.transpose(jnp.broadcast_to(sk1.astype(F32), (128, K)))
    loc_s2.wait()
    one_hot(sk2v[0, pl.ds(b // 4, 1), :], p2)
    ag1.got(18)
    ag1.go(21, 23)
    ag1.got(19)
    ag1.go(22, 24)
    ag1.got(9)
    ag1.go(12, 13)
    ag1.hand(1)
    ag1.got(10)
    ag1.go(14)
    ag1.hand(2)
    ag1.got(11)
    ag1.go(15)
    ag1.hand(3)
    ag1.got(0)
    ag1.go(3, 4)
    ag1.got(1)
    ag1.go(5)
    ag1.hand(10)
    ag1.got(2)
    ag1.go(6)
    ag1.hand(11)
    ag1.got(21)
    ag1.go(25)
    ag1.got(22)
    ag1.go(26)
    t_w2i.start()
    t_w2o.start()
    ag1.got(20)
    ag1.hand(9)
    ag1.got(12)
    ag1.go(16)
    ag1.hand(4)
    ag1.got(13)
    ag1.go(17)
    ag1.hand(5)

    @pl.when(not_mid)
    def _():
        spread_side((7, 5, 3), True)

    ag1.got(3)
    ag1.go(7)
    ag1.got(4)
    ag1.go(8)

    ag1.got(23)
    ag1.hand(12)
    ag1.got(24)
    ag1.hand(13)
    ag1.together([14, 15])
    ag1.hand(6)
    ag1.together([16, 17])
    ag1.hand(7)

    @pl.when(not_mid)
    def _():
        spread_side((1, 6, 4, 2), False)

    @pl.when(mid)
    def _():
        settle(ga.at[0, 2], dr1.at[0])
        sides = (base_of(endr, c, dp, 2) - times(lh2, ga, 2)).astype(BF)
        half = p2[pl.ds(pl.multiple_of(h * K, 16), K), :]
        stg[...] = fdot(sides, half).astype(BF).reshape(2, fr, K)
        t_pick.start()

    ag1.together([5, 6])
    ag1.hand(14)
    ag1.together([25, 26])
    ag1.together([7, 8])
    ag1.hand(15)

    @pl.when(not_mid)
    def _():
        settle(ga.at[0, 2], dr1.at[0])

    settle(ga.at[0, 0:2], dr1.at[1])

    into = srow.at[f // 4, :, pl.ds(pl.multiple_of(lw * (f % 4), 128), lw)]
    dest_box = b - c + 1 - h

    def pass_w2():
        t_w2i.wait_recv()
        t_w2fi.start()
        t_w2o.wait_recv()
        t_w2fo.start()

    def side_select():
        pltpu.make_async_copy(chunk_of(f), xs.at[own_rows, :], lsem.at[2]).wait()
        pltpu.make_async_copy(sib_chunk_of(f), xs.at[sib_rows, :], lsem.at[5]).wait()
        settle(xs.at[0 : 14 * fr, :], arecv.at[0])
        lane = lax.broadcasted_iota(jnp.int32, (K, 128), 1)
        mine = skt[...].astype(jnp.int32)
        total = None
        for part in range(8):
            hot = jnp.where(mine == lane + part * 128, 1.0, 0.0).astype(BF)
            term = fdot(hot, xs[part * 128 : (part + 1) * 128, :])
            total = term if total is None else total + term
        sel[...] = total.astype(BF)
        for d in (7, 5, 3, 1, 6, 4, 2, 0):
            rows = pl.ds(pl.multiple_of((f ^ d) * fr, 16), fr)
            remote(sel.at[rows, :], into, bsend.at[0], brecv.at[0], (dest_box, f ^ d)).start()

    def level_two():
        loc_w2.wait()
        t_w2.wait_recv()
        t_w2fi.wait_recv()
        t_w2fo.wait_recv()
        coupled(r2, h, lh, lh2, wb, p2, dp)

    def third(i):
        ag2.got(8 + 4 * i)
        ag2.go(10 + 4 * i)
        ag2.hand(2 * (8 + i))
        ag2.got(9 + 4 * i)
        ag2.go(11 + 4 * i)
        ag2.hand(2 * (4 + i))
        ag2.got(24 + 4 * i)
        ag2.go(26 + 4 * i)
        ag2.hand(2 * (4 * i + 1) + 1)
        ag2.got(25 + 4 * i)
        ag2.go(27 + 4 * i)
        ag2.hand(2 * (4 * i + 2) + 1)

    def finish(block):
        value = base_of(r2, h, dp, block) - times(lh2, gt, block)
        out[:, 0, :, block * K : (block + 1) * K] = value.astype(BF).reshape(2, fr, K)

    @pl.when(mid)
    def _():
        ends = fdot(lh2[...], ga[h, 0:2].reshape(2 * K, K))
        gt[h, 0:2, face_rows, :] = (-ends).astype(BF).reshape(2, fr, K)
        ag2.start(0)
        ag2.start(1)
        t_pick.wait_recv()
        gt[h, 2, face_rows, :] = stg[h] + pex[...]
        ag2.start(2)
        ag2.start(3)
        pass_w2()
        ag2.near(0)
        ag2.near(1)
        ag2.turn(0, 0)
        ag2.turn(1, 0)
        ag2.near(2)
        ag2.near(3)
        ag2.two_away(0)
        ag2.two_away(1)
        ag2.turn(2, 0)
        ag2.turn(3, 0)
        ag2.turn(0, 1)
        ag2.turn(1, 1)
        ag2.two_away(2)
        ag2.two_away(3)
        ag2.turn(0, 2)
        ag2.turn(1, 2)

        ag2.turn(2, 1)
        ag2.turn(3, 1)
        ag2.turn(0, 3)
        ag2.turn(1, 3)
        for i in (2, 3):
            ag2.turn(2, i)
            ag2.turn(3, i)
        settle(srow, brecv.at[0])
        seen = skt[face_rows, :]
        left1 = jnp.tile(jnp.where(seen < K, 1.0, 0.0), (1, 4)).astype(BF)
        right1 = 1 - left1
        left = jnp.concatenate([left1, left1], axis=0)
        right = 1 - left
        couple = [srow[t, :, K : 2 * K] * left1 + srow[t, :, 0:K] * right1 for t in range(2)]
        write_left(lhs_s, couple[0], couple[1])
        hid = fdot(lhs_s[...], wa[...].reshape(2 * K, K)).astype(BF)
        write_left(lh2_s, hid[:fr], hid[fr:])
        sides = srow[:, :, 2 * K :].reshape(2 * fr, K)
        dps[...] = (fdot(sides * left, p1[0:K, :]) + fdot(sides * right, p1[K:, :])).astype(BF)
        for block in (2, 0, 1):
            if block == 2:
                base = dps[...].astype(F32)
            else:
                on = left if block == 0 else right
                base = (srow[:, :, block * K : (block + 1) * K].reshape(2 * fr, K) * on).astype(F32)
            value = base - times(lh2_s, ga, block)
            r2[:, :, block * K : (block + 1) * K] = value.astype(BF).reshape(2, fr, K)

        level_two()
        ag2.corners(0)
        ag2.corners(1)
        ag2.last_corner(0)
        ag2.last_corner(1)
        finish(0)
        finish(1)
        ag2.corners(2)
        ag2.corners(3)
        ag2.last_corner(2)
        ag2.last_corner(3)

    @pl.when(not_mid)
    def _():
        for block in (2, 0, 1):
            value = base_of(endr, c, dp, block) - times(lh2, ga, block)
            r2[:, :, block * K : (block + 1) * K] = value.astype(BF).reshape(2, fr, K)
        pass_w2()
        side_select()
        level_two()
        settle(gt.at[:, 0:2], dr2.at[0])
        finish(0)
        finish(1)
        settle(gt.at[:, 2], dr2.at[1])

    finish(2)

    settle(ga.at[0, :, 0 : 7 * fr, :], ssem.at[0])
    settle(ga.at[0, :, 0 : 7 * fr, :], s1.at[0])
    settle(ga.at[0], ds1.at[0])

    @pl.when(mid)
    def _():
        settle(ga.at[0, 0, 0 : 7 * fr, :], ssem.at[1])
        settle(gt.at[:, :, 0 : K - fr // 2, :], s2.at[0])
        settle(gt, ds2.at[0])

    @pl.when(not_mid)
    def _():
        settle(sel, bsend.at[0])
        settle(xs.at[0 : 14 * fr, :], asend.at[0])


def on_device(leaf, w1, w2, skel1, skel2):
    fr = leaf.shape[4]
    hbm_spec = pl.BlockSpec(memory_space=pltpu.HBM)
    dma = pltpu.SemaphoreType.DMA
    lw = 3 * 2 * K // 8
    scratch = [
        pltpu.VMEM(skel1.shape, jnp.int32),
        pltpu.VMEM(skel2.shape, jnp.int32),
        pltpu.VMEM((2, fr, K), BF),
        pltpu.VMEM((2, fr, 3 * K), BF),
        pltpu.VMEM((2, fr, 3 * K), BF),
        pltpu.VMEM((2 * K, lw), BF),
        pltpu.VMEM((K, lw), BF),
        pltpu.VMEM((2, fr, 3 * K), BF),
        pltpu.VMEM((2 * K, K), BF),
        pltpu.VMEM((2 * K, K), BF),
        pltpu.VMEM((K, 128), F32),
        pltpu.VMEM((2, K, K), BF),
        pltpu.VMEM((2, K, K), BF),
        pltpu.VMEM((2, 3, K, K), BF),
        pltpu.VMEM((2, 3, K, K), BF),
        pltpu.VMEM((2 * fr, 2 * K), BF),
        pltpu.VMEM((2 * fr, 2 * K), BF),
        pltpu.VMEM((2 * fr, 2 * K), BF),
        pltpu.VMEM((2 * fr, 2 * K), BF),
        pltpu.VMEM((2 * fr, K), BF),
        pltpu.VMEM((2 * fr, K), BF),
        pltpu.VMEM((2, fr, 3 * K), BF),
        pltpu.VMEM((2, fr, K), BF),
        pltpu.VMEM((fr, K), BF),
        dma((8,)),
        dma((2,)),
        dma((9,)),
        dma((1,)),
        dma((22,)),
        dma((1,)),
        dma((2,)),
        dma((1,)),
        dma((52,)),
        dma((1,)),
        dma((2,)),
        dma((1,)),
        dma((1,)),
        dma((1,)),
        dma((1,)),
    ]
    return pl.pallas_call(
        functools.partial(kernel, fr),
        out_shape=jax.ShapeDtypeStruct((2, 1, fr, 3 * K), BF),
        in_specs=[hbm_spec] * 5,
        out_specs=pl.BlockSpec(memory_space=pltpu.VMEM),
        scratch_shapes=scratch,
        compiler_params=pltpu.CompilerParams(
            collective_id=0, has_side_effects=True, vmem_limit_bytes=GRANT
        ),
    )(*[pltpu.with_memory_space_constraint(a, pltpu.HBM) for a in (leaf, w1, w2, skel1, skel2)])


def solution(mesh):
    return jax.shard_map(
        on_device,
        mesh=mesh,
        in_specs=(
            P(None, None, "box", None, "face", None),
            P(None, None, "box", None),
            P(None, None, "box", None),
            P(),
            P(),
        ),
        out_specs=P(None, None, ("box", "face"), None),
        check_vma=False,
    )
```

```python
import functools

import jax
import jax.numpy as jnp
from jax import lax
from jax.experimental import pallas as pl
from jax.experimental.pallas import tpu as pltpu
from jax.sharding import PartitionSpec as P

K = 512
BF = jnp.bfloat16
F32 = jnp.float32
MESH = pl.DeviceIdType.MESH
GRANT = 48 * 1024 * 1024


def fdot(a, b):
    return jnp.dot(a, b, preferred_element_type=F32)


def remote(src, dst, send, recv, target):
    return pltpu.make_async_remote_copy(
        src_ref=src, dst_ref=dst, send_sem=send, recv_sem=recv, device_id=target, device_id_type=MESH
    )


def write_left(ref, real, imag):
    n = real.shape[0]
    ref[0:n, 0:K] = real
    ref[0:n, K : 2 * K] = -imag
    ref[n : 2 * n, 0:K] = imag
    ref[n : 2 * n, K : 2 * K] = real


class Gather:
    def __init__(self, view, send, recv, dsend, drecv, sib):
        self.view, self.send, self.recv, self.dsend, self.drecv, self.sib = view, send, recv, dsend, drecv, sib
        self.hops, self.hands, self.split, self.shared = [], [], 8, []

    def hop(self, k):
        what, to = self.hops[k]
        ref = self.view(*what)
        return remote(ref, ref, self.send.at[0], self.recv.at[self.sem_of(k)], to)

    def together(self, slots):
        settle(self.same_bytes(slots, len(slots)), self.recv.at[self.sem_of(slots[0])])

    def hand_over(self, k):
        ref = self.view(*self.hands[k])
        return remote(ref, ref, self.dsend.at[0], self.drecv.at[k // self.split], self.sib)

    def sem_of(self, k):
        first = {slot: group[0] for group in self.shared for slot in group}
        used = [slot for slot in range(len(self.hops)) if first.get(slot, slot) == slot]
        return used.index(first.get(k, k))

    def got(self, *ks):
        for k in ks:
            self.hop(k).wait_recv()

    def go(self, *ks):
        for k in ks:
            self.hop(k).start()

    def hand(self, *ks):
        for k in ks:
            self.hand_over(k).start()


def settle(view, sem):
    pltpu.make_async_copy(view, view, sem).wait()


def face_gather(view, sems, b, f, c, sib):
    g = Gather(view, *sems, sib)
    y, xh = f // 2, f % 2

    def at(dy, dx):
        return (c, ((y + dy) % 4) * 2 + (xh + dx) % 2)

    own, up, down, far = at(0, 0), at(1, 0), at(3, 0), at(2, 0)
    side, up_side, down_side, far_side = at(0, 1), at(1, 1), at(3, 1), at(2, 1)
    lo, hi, full = (0, K // 2), (K // 2, K // 2), (0, K)
    x, u, d = (b, side[1]), (b, up[1]), (b, down[1])
    for piece in ((0, 1), (2, 1)):
        g.hops += [
            ((own, piece, full), x),
            ((own, piece, full), u),
            ((own, piece, full), d),
            ((side, piece, full), u),
            ((side, piece, full), d),
            ((down, piece, lo), u),
            ((up, piece, hi), d),
            ((down_side, piece, lo), u),
            ((up_side, piece, hi), d),
        ]
    piece = (1, 1)
    g.hops += [
        ((own, piece, full), u),
        ((own, piece, full), d),
        ((own, piece, full), x),
        ((down, piece, lo), u),
        ((up, piece, hi), d),
        ((down, piece, full), x),
        ((up, piece, full), x),
        ((far, piece, lo), x),
        ((far, piece, hi), x),
    ]
    ends, picked = (0, 2), (2, 1)
    places = (own, side, down, up, down_side, up_side, far, far_side)
    g.shared = [[5, 6], [7, 8], [14, 15], [16, 17], [25, 26]]
    g.hands = [(place, picked, full) for place in places] + [(place, ends, full) for place in places]
    return g


class Plane(Gather):
    def __init__(self, view, sems, b, f, h, cross_box, sib, fr):
        super().__init__(view, *sems, sib)
        self.split = 32
        y, xh = f // 2, f % 2

        def face(dy, dx):
            return ((y + dy) % 4) * 2 + (xh + dx) % 2

        xs = [(h, 0), (1 - h, 0), (1 - h, 1), (h, 1)]
        ys = [0, 1, 3, 2]

        def node(iy, ix):
            return (xs[ix][0], face(ys[iy], xs[ix][1]))

        lo, hi, full = (0, K // 2), (K // 2, K // 2), (0, K)
        inner, outer = (cross_box, f), (cross_box, face(0, 1))
        up, down = (b, face(1, 0)), (b, face(3, 0))
        for p, piece in enumerate(((0, 0, fr), (1, 0, fr), (2, 0, fr // 2), (2, fr // 2, fr // 2))):

            def line_x():
                return [(own, inner), (own, outer), (own, (b, face(0, 1)))]

            def line_y():
                return [(own, up), (own, down), (own, (b, face(2, 0)))]

            def round_x(iy):
                return [
                    ((node(iy, 0), piece, full), inner),
                    ((node(iy, 0), piece, full), outer),
                    ((node(iy, 1), piece, lo), outer),
                    ((node(iy, 2), piece, hi), inner),
                ]

            def round_y(ix):
                return [
                    ((node(0, ix), piece, full), up),
                    ((node(0, ix), piece, full), down),
                    ((node(2, ix), piece, lo), up),
                    ((node(1, ix), piece, hi), down),
                ]

            own = (node(0, 0), piece, full)
            first, second = (line_x, round_y) if p % 2 == 0 else (line_y, round_x)
            self.hops += first()
            for i in range(4):
                self.hops += second(i)
            self.hands += [(node(i // 4, i % 4), piece, full) for i in range(16)]
            k = 19 * p + 5
            self.shared += [[k, k + 1, k + 4, k + 5, k + 8, k + 9], [k + 12, k + 13]]

    def give(self, p, along, across):
        iy, ix = (across, along) if p % 2 == 0 else (along, across)
        self.hand(16 * p + 4 * iy + ix)

    def start(self, p):
        k = 19 * p
        self.go(k, k + 1, k + 2, k + 3, k + 4)
        self.give(p, 0, 0)

    def near(self, p):
        k = 19 * p
        for slot in (0, 1):
            place = 1 + slot if p % 2 == 0 else 2 - slot
            self.got(k + slot)
            self.go(k + 3 + 4 * place, k + 4 + 4 * place)
            self.give(p, place, 0)

    def two_away(self, p):
        k = 19 * p
        self.got(k + 2)
        self.go(k + 15, k + 16)
        self.give(p, 3, 0)

    def turn(self, p, i):
        k = 19 * p + 3 + 4 * i
        for slot in (0, 1):
            self.got(k + slot)
            self.go(k + 2 + slot)
            self.give(p, i, 2 - slot if p % 2 == 0 else 1 + slot)

    def corners(self, p):
        k = 19 * p + 5
        self.together([k, k + 1, k + 4, k + 5, k + 8, k + 9])
        for i in range(3):
            self.give(p, i, 3)

    def last_corner(self, p):
        k = 19 * p + 17
        self.together([k, k + 1])
        self.give(p, 3, 3)


def kernel(fr, leaf, w1, w2, skel1, skel2, out, sk1v, sk2v, ifs, endr, sraw, xs, sel, srow, p1, p2, skt, wa, wb, ga, gt,
           lh, lh2, lhs_s, lh2_s, dp, dps, r2, stg, pex, lsem, ssem, rsem, s1, r1, ds1, dr1, s2, r2s, ds2, dr2,
           asend, arecv, bsend, brecv):
    b, f = lax.axis_index("box"), lax.axis_index("face")
    c, h = b % 2, (b // 2) % 2
    q = b % 4
    sib = (b + 1 - 2 * c, f)
    inner_box = b + 2 - 4 * h
    other_face = f // 2 * 2 + 1 - f % 2
    inner, outer = (inner_box, f), (inner_box, other_face)
    cross_box = inner_box + 1 - 2 * c
    mid = c != h
    not_mid = jnp.logical_not(mid)

    barrier = pltpu.get_barrier_semaphore()
    up, down = (f + 2) % 8, (f + 6) % 8
    peers = [(b, up), (b, down), (b, other_face), sib, inner, outer, (cross_box, f), (cross_box, other_face)]
    for peer in peers:
        pl.semaphore_signal(barrier, inc=1, device_id=peer, device_id_type=MESH)

    def local(k, src, dst):
        copy = pltpu.make_async_copy(src, dst, lsem.at[k])
        copy.start()
        return copy

    loc_s1 = local(5, skel1, sk1v)
    loc_s2 = local(6, skel2, sk2v)
    lw = 3 * 2 * K // 8
    face_rows = pl.ds(pl.multiple_of(f * fr, 16), fr)
    own_rows = pl.ds(pl.multiple_of(c * K + f * fr, 16), fr)
    own_cols = pl.ds(pl.multiple_of(c * K, 128), K)
    loc_ga = local(7, leaf.at[:, 0, 0, 1 - c, :, own_cols], ga.at[c, 0:2, face_rows, :])
    loc_if = local(0, leaf.at[c, 0, 0, 1 - c, :, 2 * K : 3 * K], ifs.at[c])
    loc_end = local(1, leaf.at[:, 0, 0, c], endr)

    def chunk_of(j):
        return leaf.at[j // 4, 0, 0, 2, :, pl.ds(pl.multiple_of(lw * (j % 4), 128), lw)]


    @pl.when(not_mid)
    def _():
        pltpu.make_async_copy(chunk_of(f), xs.at[own_rows, :], lsem.at[2]).start()

    sib_rows = pl.ds(pl.multiple_of((1 - c) * K + f * fr, 16), fr)

    w1_rows = pl.ds(pl.multiple_of(c * (K // 2), 16), K // 2)
    w2_rows = pl.ds(pl.multiple_of(q * (K // 4), 16), K // 4)
    loc_w1 = local(3, w1.at[:, 0], wa.at[:, w1_rows, :])
    loc_w2 = local(4, w2.at[:, 0], wb.at[:, w2_rows, :])

    loc_ga.wait()

    pl.semaphore_wait(barrier, len(peers))

    t_if = remote(leaf.at[1 - c, 0, 0, 1 - c, :, 2 * K : 3 * K], ifs.at[c], ssem.at[0], rsem.at[0], sib)
    t_w1 = remote(w1.at[:, 0], wa.at[:, w1_rows, :], ssem.at[0], rsem.at[1], sib)
    t_w2 = remote(w2.at[:, 0], wb.at[:, w2_rows, :], ssem.at[0], rsem.at[2], sib)
    t_w2i = remote(w2.at[0, 0], wb.at[0, w2_rows, :], ssem.at[0], rsem.at[3], inner)
    t_w2o = remote(w2.at[1, 0], wb.at[1, w2_rows, :], ssem.at[0], rsem.at[4], outer)
    q2 = pl.ds(pl.multiple_of((q + 2 - 4 * h) * (K // 4), 16), K // 4)
    t_w2fi = remote(wb.at[0, q2, :], wb.at[0, q2, :], ssem.at[0], rsem.at[5], sib)
    t_w2fo = remote(wb.at[1, q2, :], wb.at[1, q2, :], ssem.at[0], rsem.at[6], sib)
    t_side = remote(leaf.at[:, 0, 0, 2], sraw, ssem.at[1], rsem.at[7], sib)
    t_pick = remote(stg.at[1 - h], pex, ssem.at[1], rsem.at[8], (cross_box, f))
    picker_box = b - c + h

    def sib_chunk_of(j):
        return sraw.at[j // 4, :, pl.ds(pl.multiple_of(lw * (j % 4), 128), lw)]

    def spread_side(places, first):
        if first:
            t_side.wait_recv()
            pltpu.make_async_copy(sib_chunk_of(f), xs.at[sib_rows, :], lsem.at[5]).start()
        for d in places:
            to = (picker_box, f ^ d)
            remote(chunk_of(f ^ d), xs.at[own_rows, :], asend.at[0], arecv.at[0], to).start()
            remote(sib_chunk_of(f ^ d), xs.at[sib_rows, :], asend.at[0], arecv.at[0], to).start()

    def part_rows(node, blocks, cols):
        rows = pl.ds(pl.multiple_of(node[1] * fr, 16), fr)
        return ga.at[node[0], blocks[0] : blocks[0] + blocks[1], rows, cols[0] : cols[0] + cols[1]]

    def plane_rows(node, piece, cols):
        block, at, n = piece
        return gt.at[node[0], block, pl.ds(pl.multiple_of(node[1] * fr + at, 16), n), cols[0] : cols[0] + cols[1]]

    def half_ga(slots, n):
        return ga.at[0, 0, 0 : n * fr // 2, :]

    def half_gt(slots, n):
        rows = fr if slots[0] < 38 else fr // 2
        return gt.at[0, 0, 0 : n * rows // 2, :]

    ag1 = face_gather(part_rows, (s1, r1, ds1, dr1), b, f, c, sib)
    ag2 = Plane(plane_rows, (s2, r2s, ds2, dr2), b, f, h, cross_box, sib, fr)
    ag1.same_bytes, ag2.same_bytes = half_ga, half_gt

    t_if.start()
    ag1.go(18, 19, 0)
    ag1.hand(8)
    t_w1.start()
    t_w2.start()

    @pl.when(mid)
    def _():
        t_side.start()


    def one_hot(rows, pick):
        for part in range(4):
            at = part * 256
            index = lax.broadcasted_iota(jnp.int32, (256, K), 0) + at
            pick[at : at + 256, :] = jnp.where(index == rows, 1.0, 0.0).astype(BF)

    loc_s1.wait()
    sk1 = sk1v[0, pl.ds(b // 2, 1), :]
    one_hot(sk1, p1)
    loc_if.wait()
    t_if.wait_recv()
    ga[c, 2, face_rows, :] = (fdot(ifs[0], p1[0:K, :]) + fdot(ifs[1], p1[K:, :])).astype(BF)
    ag1.go(9, 10, 11, 1, 2, 20)
    ag1.hand(0)

    def coupled(rows, side, left, left2, weights, pick, dest):
        couple = rows[:, :, pl.ds(pl.multiple_of((1 - side) * K, 128), K)]
        write_left(left, couple[0], couple[1])
        hid = fdot(left[...], weights[...].reshape(2 * K, K)).astype(BF)
        write_left(left2, hid[:fr], hid[fr:])
        side_cols = rows[:, :, 2 * K :].reshape(2 * fr, K)
        half = pick[pl.ds(pl.multiple_of(side * K, 16), K), :]
        dest[...] = fdot(side_cols, half).astype(BF)

    def base_of(rows, side, dest, block):
        if block == 2:
            return dest[...].astype(F32)
        on = jnp.where(side == block, 1.0, 0.0)
        return rows[:, :, block * K : (block + 1) * K].reshape(2 * fr, K).astype(F32) * on

    def times(left2, gathered, block):
        if block == 2:
            left = left2[...]
            return fdot(left[:, :K], gathered[0, 2]) + fdot(left[:, K:], gathered[1, 2])
        return fdot(left2[...], gathered[block, 0:2].reshape(2 * K, K))

    loc_end.wait()
    loc_w1.wait()
    t_w1.wait_recv()
    coupled(endr, c, lh, lh2, wa, p1, dp)

    skt[...] = jnp.transpose(jnp.broadcast_to(sk1.astype(F32), (128, K)))
    loc_s2.wait()
    one_hot(sk2v[0, pl.ds(b // 4, 1), :], p2)
    ag1.got(18)
    ag1.go(21, 23)
    ag1.got(19)
    ag1.go(22, 24)
    ag1.got(9)
    ag1.go(12, 13)
    ag1.hand(1)
    ag1.got(10)
    ag1.go(14)
    ag1.hand(2)
    ag1.got(11)
    ag1.go(15)
    ag1.hand(3)
    ag1.got(0)
    ag1.go(3, 4)
    ag1.got(1)
    ag1.go(5)
    ag1.hand(10)
    ag1.got(2)
    ag1.go(6)
    ag1.hand(11)
    ag1.got(21)
    ag1.go(25)
    ag1.got(22)
    ag1.go(26)
    t_w2i.start()
    t_w2o.start()
    ag1.got(20)
    ag1.hand(9)
    ag1.got(12)
    ag1.go(16)
    ag1.hand(4)
    ag1.got(13)
    ag1.go(17)
    ag1.hand(5)

    @pl.when(not_mid)
    def _():
        spread_side((3, 1), True)

    ag1.got(3)
    ag1.go(7)
    ag1.got(4)
    ag1.go(8)

    ag1.got(23)
    ag1.hand(12)
    ag1.got(24)
    ag1.hand(13)
    ag1.together([14, 15])
    ag1.hand(6)
    ag1.together([16, 17])
    ag1.hand(7)

    @pl.when(not_mid)
    def _():
        spread_side((7, 5, 6, 4, 2), False)

    @pl.when(mid)
    def _():
        settle(ga.at[0, 2], dr1.at[0])
        sides = (base_of(endr, c, dp, 2) - times(lh2, ga, 2)).astype(BF)
        half = p2[pl.ds(pl.multiple_of(h * K, 16), K), :]
        stg[...] = fdot(sides, half).astype(BF).reshape(2, fr, K)
        t_pick.start()

    ag1.together([5, 6])
    ag1.hand(14)
    ag1.together([25, 26])
    ag1.together([7, 8])
    ag1.hand(15)

    @pl.when(not_mid)
    def _():
        settle(ga.at[0, 2], dr1.at[0])

    settle(ga.at[0, 0:2], dr1.at[1])

    into = srow.at[f // 4, :, pl.ds(pl.multiple_of(lw * (f % 4), 128), lw)]
    dest_box = b - c + 1 - h

    def pass_w2():
        t_w2i.wait_recv()
        t_w2fi.start()
        t_w2o.wait_recv()
        t_w2fo.start()

    def side_select():
        pltpu.make_async_copy(chunk_of(f), xs.at[own_rows, :], lsem.at[2]).wait()
        pltpu.make_async_copy(sib_chunk_of(f), xs.at[sib_rows, :], lsem.at[5]).wait()
        settle(xs.at[0 : 14 * fr, :], arecv.at[0])
        lane = lax.broadcasted_iota(jnp.int32, (K, 128), 1)
        mine = skt[...].astype(jnp.int32)
        total = None
        for part in range(8):
            hot = jnp.where(mine == lane + part * 128, 1.0, 0.0).astype(BF)
            term = fdot(hot, xs[part * 128 : (part + 1) * 128, :])
            total = term if total is None else total + term
        sel[...] = total.astype(BF)
        for d in (7, 5, 3, 1, 6, 4, 2, 0):
            rows = pl.ds(pl.multiple_of((f ^ d) * fr, 16), fr)
            remote(sel.at[rows, :], into, bsend.at[0], brecv.at[0], (dest_box, f ^ d)).start()

    def level_two():
        loc_w2.wait()
        t_w2.wait_recv()
        t_w2fi.wait_recv()
        t_w2fo.wait_recv()
        coupled(r2, h, lh, lh2, wb, p2, dp)

    def third(i):
        ag2.got(8 + 4 * i)
        ag2.go(10 + 4 * i)
        ag2.hand(2 * (8 + i))
        ag2.got(9 + 4 * i)
        ag2.go(11 + 4 * i)
        ag2.hand(2 * (4 + i))
        ag2.got(24 + 4 * i)
        ag2.go(26 + 4 * i)
        ag2.hand(2 * (4 * i + 1) + 1)
        ag2.got(25 + 4 * i)
        ag2.go(27 + 4 * i)
        ag2.hand(2 * (4 * i + 2) + 1)

    def finish(block):
        value = base_of(r2, h, dp, block) - times(lh2, gt, block)
        out[:, 0, :, block * K : (block + 1) * K] = value.astype(BF).reshape(2, fr, K)

    @pl.when(mid)
    def _():
        ends = fdot(lh2[...], ga[h, 0:2].reshape(2 * K, K))
        gt[h, 0:2, face_rows, :] = (-ends).astype(BF).reshape(2, fr, K)
        ag2.start(0)
        ag2.start(1)
        t_pick.wait_recv()
        gt[h, 2, face_rows, :] = stg[h] + pex[...]
        ag2.start(2)
        ag2.start(3)
        pass_w2()
        ag2.near(0)
        ag2.near(1)
        ag2.turn(0, 0)
        ag2.turn(1, 0)
        ag2.near(2)
        ag2.near(3)
        ag2.two_away(0)
        ag2.two_away(1)
        ag2.turn(2, 0)
        ag2.turn(3, 0)
        ag2.turn(0, 1)
        ag2.turn(1, 1)
        ag2.two_away(2)
        ag2.two_away(3)
        ag2.turn(0, 2)
        ag2.turn(1, 2)

        ag2.turn(2, 1)
        ag2.turn(3, 1)
        ag2.turn(0, 3)
        ag2.turn(1, 3)
        for i in (2, 3):
            ag2.turn(2, i)
            ag2.turn(3, i)
        settle(srow, brecv.at[0])
        seen = skt[face_rows, :]
        left1 = jnp.tile(jnp.where(seen < K, 1.0, 0.0), (1, 4)).astype(BF)
        right1 = 1 - left1
        left = jnp.concatenate([left1, left1], axis=0)
        right = 1 - left
        couple = [srow[t, :, K : 2 * K] * left1 + srow[t, :, 0:K] * right1 for t in range(2)]
        write_left(lhs_s, couple[0], couple[1])
        hid = fdot(lhs_s[...], wa[...].reshape(2 * K, K)).astype(BF)
        write_left(lh2_s, hid[:fr], hid[fr:])
        sides = srow[:, :, 2 * K :].reshape(2 * fr, K)
        dps[...] = (fdot(sides * left, p1[0:K, :]) + fdot(sides * right, p1[K:, :])).astype(BF)
        for block in (2, 0, 1):
            if block == 2:
                base = dps[...].astype(F32)
            else:
                on = left if block == 0 else right
                base = (srow[:, :, block * K : (block + 1) * K].reshape(2 * fr, K) * on).astype(F32)
            value = base - times(lh2_s, ga, block)
            r2[:, :, block * K : (block + 1) * K] = value.astype(BF).reshape(2, fr, K)

        level_two()
        ag2.corners(0)
        ag2.corners(1)
        ag2.last_corner(0)
        ag2.last_corner(1)
        finish(0)
        finish(1)
        ag2.corners(2)
        ag2.corners(3)
        ag2.last_corner(2)
        ag2.last_corner(3)

    @pl.when(not_mid)
    def _():
        for block in (2, 0, 1):
            value = base_of(endr, c, dp, block) - times(lh2, ga, block)
            r2[:, :, block * K : (block + 1) * K] = value.astype(BF).reshape(2, fr, K)
        pass_w2()
        side_select()
        level_two()
        settle(gt.at[:, 0:2], dr2.at[0])
        finish(0)
        finish(1)
        settle(gt.at[:, 2], dr2.at[1])

    finish(2)

    settle(ga.at[0, :, 0 : 7 * fr, :], ssem.at[0])
    settle(ga.at[0, :, 0 : 7 * fr, :], s1.at[0])
    settle(ga.at[0], ds1.at[0])

    @pl.when(mid)
    def _():
        settle(ga.at[0, 0, 0 : 7 * fr, :], ssem.at[1])
        settle(gt.at[:, :, 0 : K - fr // 2, :], s2.at[0])
        settle(gt, ds2.at[0])

    @pl.when(not_mid)
    def _():
        settle(sel, bsend.at[0])
        settle(xs.at[0 : 14 * fr, :], asend.at[0])


def on_device(leaf, w1, w2, skel1, skel2):
    fr = leaf.shape[4]
    hbm_spec = pl.BlockSpec(memory_space=pltpu.HBM)
    dma = pltpu.SemaphoreType.DMA
    lw = 3 * 2 * K // 8
    scratch = [
        pltpu.VMEM(skel1.shape, jnp.int32),
        pltpu.VMEM(skel2.shape, jnp.int32),
        pltpu.VMEM((2, fr, K), BF),
        pltpu.VMEM((2, fr, 3 * K), BF),
        pltpu.VMEM((2, fr, 3 * K), BF),
        pltpu.VMEM((2 * K, lw), BF),
        pltpu.VMEM((K, lw), BF),
        pltpu.VMEM((2, fr, 3 * K), BF),
        pltpu.VMEM((2 * K, K), BF),
        pltpu.VMEM((2 * K, K), BF),
        pltpu.VMEM((K, 128), F32),
        pltpu.VMEM((2, K, K), BF),
        pltpu.VMEM((2, K, K), BF),
        pltpu.VMEM((2, 3, K, K), BF),
        pltpu.VMEM((2, 3, K, K), BF),
        pltpu.VMEM((2 * fr, 2 * K), BF),
        pltpu.VMEM((2 * fr, 2 * K), BF),
        pltpu.VMEM((2 * fr, 2 * K), BF),
        pltpu.VMEM((2 * fr, 2 * K), BF),
        pltpu.VMEM((2 * fr, K), BF),
        pltpu.VMEM((2 * fr, K), BF),
        pltpu.VMEM((2, fr, 3 * K), BF),
        pltpu.VMEM((2, fr, K), BF),
        pltpu.VMEM((fr, K), BF),
        dma((8,)),
        dma((2,)),
        dma((9,)),
        dma((1,)),
        dma((22,)),
        dma((1,)),
        dma((2,)),
        dma((1,)),
        dma((52,)),
        dma((1,)),
        dma((2,)),
        dma((1,)),
        dma((1,)),
        dma((1,)),
        dma((1,)),
    ]
    return pl.pallas_call(
        functools.partial(kernel, fr),
        out_shape=jax.ShapeDtypeStruct((2, 1, fr, 3 * K), BF),
        in_specs=[hbm_spec] * 5,
        out_specs=pl.BlockSpec(memory_space=pltpu.VMEM),
        scratch_shapes=scratch,
        compiler_params=pltpu.CompilerParams(
            collective_id=0, has_side_effects=True, vmem_limit_bytes=GRANT
        ),
    )(*[pltpu.with_memory_space_constraint(a, pltpu.HBM) for a in (leaf, w1, w2, skel1, skel2)])


def solution(mesh):
    return jax.shard_map(
        on_device,
        mesh=mesh,
        in_specs=(
            P(None, None, "box", None, "face", None),
            P(None, None, "box", None),
            P(None, None, "box", None),
            P(),
            P(),
        ),
        out_specs=P(None, None, ("box", "face"), None),
        check_vma=False,
    )
```

```python
import functools

import jax
import jax.numpy as jnp
from jax import lax
from jax.experimental import pallas as pl
from jax.experimental.pallas import tpu as pltpu
from jax.sharding import PartitionSpec as P

K = 512
BF = jnp.bfloat16
F32 = jnp.float32
MESH = pl.DeviceIdType.MESH
GRANT = 48 * 1024 * 1024


def fdot(a, b):
    return jnp.dot(a, b, preferred_element_type=F32)


def remote(src, dst, send, recv, target):
    return pltpu.make_async_remote_copy(
        src_ref=src, dst_ref=dst, send_sem=send, recv_sem=recv, device_id=target, device_id_type=MESH
    )


def write_left(ref, real, imag):
    n = real.shape[0]
    ref[0:n, 0:K] = real
    ref[0:n, K : 2 * K] = -imag
    ref[n : 2 * n, 0:K] = imag
    ref[n : 2 * n, K : 2 * K] = real


class Gather:
    def __init__(self, view, send, recv, dsend, drecv, sib):
        self.view, self.send, self.recv, self.dsend, self.drecv, self.sib = view, send, recv, dsend, drecv, sib
        self.hops, self.hands, self.split, self.shared = [], [], 8, []

    def hop(self, k):
        what, to = self.hops[k]
        ref = self.view(*what)
        return remote(ref, ref, self.send.at[0], self.recv.at[self.sem_of(k)], to)

    def together(self, slots):
        settle(self.same_bytes(slots, len(slots)), self.recv.at[self.sem_of(slots[0])])

    def hand_over(self, k):
        ref = self.view(*self.hands[k])
        return remote(ref, ref, self.dsend.at[0], self.drecv.at[k // self.split], self.sib)

    def sem_of(self, k):
        first = {slot: group[0] for group in self.shared for slot in group}
        used = [slot for slot in range(len(self.hops)) if first.get(slot, slot) == slot]
        return used.index(first.get(k, k))

    def got(self, *ks):
        for k in ks:
            self.hop(k).wait_recv()

    def go(self, *ks):
        for k in ks:
            self.hop(k).start()

    def hand(self, *ks):
        for k in ks:
            self.hand_over(k).start()


def settle(view, sem):
    pltpu.make_async_copy(view, view, sem).wait()


def face_gather(view, sems, b, f, c, sib):
    g = Gather(view, *sems, sib)
    y, xh = f // 2, f % 2

    def at(dy, dx):
        return (c, ((y + dy) % 4) * 2 + (xh + dx) % 2)

    own, up, down, far = at(0, 0), at(1, 0), at(3, 0), at(2, 0)
    side, up_side, down_side, far_side = at(0, 1), at(1, 1), at(3, 1), at(2, 1)
    lo, hi, full = (0, K // 2), (K // 2, K // 2), (0, K)
    x, u, d = (b, side[1]), (b, up[1]), (b, down[1])
    for piece in ((0, 1), (2, 1)):
        g.hops += [
            ((own, piece, full), x),
            ((own, piece, full), u),
            ((own, piece, full), d),
            ((side, piece, full), u),
            ((side, piece, full), d),
            ((down, piece, lo), u),
            ((up, piece, hi), d),
            ((down_side, piece, lo), u),
            ((up_side, piece, hi), d),
        ]
    piece = (1, 1)
    g.hops += [
        ((own, piece, full), u),
        ((own, piece, full), d),
        ((own, piece, full), x),
        ((down, piece, lo), u),
        ((up, piece, hi), d),
        ((down, piece, full), x),
        ((up, piece, full), x),
        ((far, piece, lo), x),
        ((far, piece, hi), x),
    ]
    ends, picked = (0, 2), (2, 1)
    places = (own, side, down, up, down_side, up_side, far, far_side)
    g.shared = [[5, 6], [7, 8], [14, 15], [16, 17], [25, 26]]
    g.hands = [(place, picked, full) for place in places] + [(place, ends, full) for place in places]
    return g


class Plane(Gather):
    def __init__(self, view, sems, b, f, h, cross_box, sib, fr):
        super().__init__(view, *sems, sib)
        self.split = 32
        y, xh = f // 2, f % 2

        def face(dy, dx):
            return ((y + dy) % 4) * 2 + (xh + dx) % 2

        xs = [(h, 0), (1 - h, 0), (1 - h, 1), (h, 1)]
        ys = [0, 1, 3, 2]

        def node(iy, ix):
            return (xs[ix][0], face(ys[iy], xs[ix][1]))

        lo, hi, full = (0, K // 2), (K // 2, K // 2), (0, K)
        inner, outer = (cross_box, f), (cross_box, face(0, 1))
        up, down = (b, face(1, 0)), (b, face(3, 0))
        for p, piece in enumerate(((0, 0, fr), (1, 0, fr), (2, 0, fr // 2), (2, fr // 2, fr // 2))):

            def line_x():
                return [(own, inner), (own, outer), (own, (b, face(0, 1)))]

            def line_y():
                return [(own, up), (own, down), (own, (b, face(2, 0)))]

            def round_x(iy):
                return [
                    ((node(iy, 0), piece, full), inner),
                    ((node(iy, 0), piece, full), outer),
                    ((node(iy, 1), piece, lo), outer),
                    ((node(iy, 2), piece, hi), inner),
                ]

            def round_y(ix):
                return [
                    ((node(0, ix), piece, full), up),
                    ((node(0, ix), piece, full), down),
                    ((node(2, ix), piece, lo), up),
                    ((node(1, ix), piece, hi), down),
                ]

            own = (node(0, 0), piece, full)
            first, second = (line_x, round_y) if p % 2 == 0 else (line_y, round_x)
            self.hops += first()
            for i in range(4):
                self.hops += second(i)
            self.hands += [(node(i // 4, i % 4), piece, full) for i in range(16)]
            k = 19 * p + 5
            self.shared += [[k, k + 1, k + 4, k + 5, k + 8, k + 9], [k + 12, k + 13]]

    def give(self, p, along, across):
        iy, ix = (across, along) if p % 2 == 0 else (along, across)
        self.hand(16 * p + 4 * iy + ix)

    def start(self, p):
        k = 19 * p
        self.go(k, k + 1, k + 2, k + 3, k + 4)
        self.give(p, 0, 0)

    def near(self, p):
        k = 19 * p
        for slot in (0, 1):
            place = 1 + slot if p % 2 == 0 else 2 - slot
            self.got(k + slot)
            self.go(k + 3 + 4 * place, k + 4 + 4 * place)
            self.give(p, place, 0)

    def two_away(self, p):
        k = 19 * p
        self.got(k + 2)
        self.go(k + 15, k + 16)
        self.give(p, 3, 0)

    def turn(self, p, i):
        k = 19 * p + 3 + 4 * i
        for slot in (0, 1):
            self.got(k + slot)
            self.go(k + 2 + slot)
            self.give(p, i, 2 - slot if p % 2 == 0 else 1 + slot)

    def corners(self, p):
        k = 19 * p + 5
        self.together([k, k + 1, k + 4, k + 5, k + 8, k + 9])
        for i in range(3):
            self.give(p, i, 3)

    def last_corner(self, p):
        k = 19 * p + 17
        self.together([k, k + 1])
        self.give(p, 3, 3)


def kernel(fr, leaf, w1, w2, skel1, skel2, out, sk1v, sk2v, ifs, endr, sraw, xs, sel, srow, p1, p2, skt, wa, wb, ga, gt,
           lh, lh2, lhs_s, lh2_s, dp, dps, r2, stg, pex, lsem, ssem, rsem, s1, r1, ds1, dr1, s2, r2s, ds2, dr2,
           asend, arecv, bsend, brecv):
    b, f = lax.axis_index("box"), lax.axis_index("face")
    c, h = b % 2, (b // 2) % 2
    q = b % 4
    sib = (b + 1 - 2 * c, f)
    inner_box = b + 2 - 4 * h
    other_face = f // 2 * 2 + 1 - f % 2
    inner, outer = (inner_box, f), (inner_box, other_face)
    cross_box = inner_box + 1 - 2 * c
    mid = c != h
    not_mid = jnp.logical_not(mid)

    barrier = pltpu.get_barrier_semaphore()
    up, down = (f + 2) % 8, (f + 6) % 8
    peers = [(b, up), (b, down), (b, other_face), sib, inner, outer, (cross_box, f), (cross_box, other_face)]
    for peer in peers:
        pl.semaphore_signal(barrier, inc=1, device_id=peer, device_id_type=MESH)

    def local(k, src, dst):
        copy = pltpu.make_async_copy(src, dst, lsem.at[k])
        copy.start()
        return copy

    loc_s1 = local(5, skel1, sk1v)
    loc_s2 = local(6, skel2, sk2v)
    lw = 3 * 2 * K // 8
    face_rows = pl.ds(pl.multiple_of(f * fr, 16), fr)
    own_rows = pl.ds(pl.multiple_of(c * K + f * fr, 16), fr)
    own_cols = pl.ds(pl.multiple_of(c * K, 128), K)
    loc_ga = local(7, leaf.at[:, 0, 0, 1 - c, :, own_cols], ga.at[c, 0:2, face_rows, :])
    loc_if = local(0, leaf.at[c, 0, 0, 1 - c, :, 2 * K : 3 * K], ifs.at[c])
    loc_end = local(1, leaf.at[:, 0, 0, c], endr)

    def chunk_of(j):
        return leaf.at[j // 4, 0, 0, 2, :, pl.ds(pl.multiple_of(lw * (j % 4), 128), lw)]


    @pl.when(not_mid)
    def _():
        pltpu.make_async_copy(chunk_of(f), xs.at[own_rows, :], lsem.at[2]).start()

    sib_rows = pl.ds(pl.multiple_of((1 - c) * K + f * fr, 16), fr)

    w1_rows = pl.ds(pl.multiple_of(c * (K // 2), 16), K // 2)
    w2_rows = pl.ds(pl.multiple_of(q * (K // 4), 16), K // 4)
    loc_w1 = local(3, w1.at[:, 0], wa.at[:, w1_rows, :])
    loc_w2 = local(4, w2.at[:, 0], wb.at[:, w2_rows, :])

    loc_ga.wait()

    pl.semaphore_wait(barrier, len(peers))

    t_if = remote(leaf.at[1 - c, 0, 0, 1 - c, :, 2 * K : 3 * K], ifs.at[c], ssem.at[0], rsem.at[0], sib)
    t_w1 = remote(w1.at[:, 0], wa.at[:, w1_rows, :], ssem.at[0], rsem.at[1], sib)
    t_w2 = remote(w2.at[:, 0], wb.at[:, w2_rows, :], ssem.at[0], rsem.at[2], sib)
    t_w2i = remote(w2.at[0, 0], wb.at[0, w2_rows, :], ssem.at[0], rsem.at[3], inner)
    t_w2o = remote(w2.at[1, 0], wb.at[1, w2_rows, :], ssem.at[0], rsem.at[4], outer)
    q2 = pl.ds(pl.multiple_of((q + 2 - 4 * h) * (K // 4), 16), K // 4)
    t_w2fi = remote(wb.at[0, q2, :], wb.at[0, q2, :], ssem.at[0], rsem.at[5], sib)
    t_w2fo = remote(wb.at[1, q2, :], wb.at[1, q2, :], ssem.at[0], rsem.at[6], sib)
    t_side = remote(leaf.at[:, 0, 0, 2], sraw, ssem.at[1], rsem.at[7], sib)
    t_pick = remote(stg.at[1 - h], pex, ssem.at[1], rsem.at[8], (cross_box, f))
    picker_box = b - c + h

    def sib_chunk_of(j):
        return sraw.at[j // 4, :, pl.ds(pl.multiple_of(lw * (j % 4), 128), lw)]

    def spread_side(places, first):
        if first:
            t_side.wait_recv()
            pltpu.make_async_copy(sib_chunk_of(f), xs.at[sib_rows, :], lsem.at[5]).start()
        for d in places:
            to = (picker_box, f ^ d)
            remote(chunk_of(f ^ d), xs.at[own_rows, :], asend.at[0], arecv.at[0], to).start()
            remote(sib_chunk_of(f ^ d), xs.at[sib_rows, :], asend.at[0], arecv.at[0], to).start()

    def part_rows(node, blocks, cols):
        rows = pl.ds(pl.multiple_of(node[1] * fr, 16), fr)
        return ga.at[node[0], blocks[0] : blocks[0] + blocks[1], rows, cols[0] : cols[0] + cols[1]]

    def plane_rows(node, piece, cols):
        block, at, n = piece
        return gt.at[node[0], block, pl.ds(pl.multiple_of(node[1] * fr + at, 16), n), cols[0] : cols[0] + cols[1]]

    def half_ga(slots, n):
        return ga.at[0, 0, 0 : n * fr // 2, :]

    def half_gt(slots, n):
        rows = fr if slots[0] < 38 else fr // 2
        return gt.at[0, 0, 0 : n * rows // 2, :]

    ag1 = face_gather(part_rows, (s1, r1, ds1, dr1), b, f, c, sib)
    ag2 = Plane(plane_rows, (s2, r2s, ds2, dr2), b, f, h, cross_box, sib, fr)
    ag1.same_bytes, ag2.same_bytes = half_ga, half_gt

    t_if.start()
    ag1.go(18, 19, 0)
    ag1.hand(8)
    t_w1.start()
    t_w2.start()

    @pl.when(mid)
    def _():
        t_side.start()


    def one_hot(rows, pick):
        for part in range(4):
            at = part * 256
            index = lax.broadcasted_iota(jnp.int32, (256, K), 0) + at
            pick[at : at + 256, :] = jnp.where(index == rows, 1.0, 0.0).astype(BF)

    loc_s1.wait()
    sk1 = sk1v[0, pl.ds(b // 2, 1), :]
    one_hot(sk1, p1)
    loc_if.wait()
    t_if.wait_recv()
    ga[c, 2, face_rows, :] = (fdot(ifs[0], p1[0:K, :]) + fdot(ifs[1], p1[K:, :])).astype(BF)
    ag1.go(9, 10, 11, 1, 2, 20)
    ag1.hand(0)

    def coupled(rows, side, left, left2, weights, pick, dest):
        couple = rows[:, :, pl.ds(pl.multiple_of((1 - side) * K, 128), K)]
        write_left(left, couple[0], couple[1])
        hid = fdot(left[...], weights[...].reshape(2 * K, K)).astype(BF)
        write_left(left2, hid[:fr], hid[fr:])
        side_cols = rows[:, :, 2 * K :].reshape(2 * fr, K)
        half = pick[pl.ds(pl.multiple_of(side * K, 16), K), :]
        dest[...] = fdot(side_cols, half).astype(BF)

    def base_of(rows, side, dest, block):
        if block == 2:
            return dest[...].astype(F32)
        on = jnp.where(side == block, 1.0, 0.0)
        return rows[:, :, block * K : (block + 1) * K].reshape(2 * fr, K).astype(F32) * on

    def times(left2, gathered, block):
        if block == 2:
            left = left2[...]
            return fdot(left[:, :K], gathered[0, 2]) + fdot(left[:, K:], gathered[1, 2])
        return fdot(left2[...], gathered[block, 0:2].reshape(2 * K, K))

    loc_end.wait()
    loc_w1.wait()
    t_w1.wait_recv()
    coupled(endr, c, lh, lh2, wa, p1, dp)

    skt[...] = jnp.transpose(jnp.broadcast_to(sk1.astype(F32), (128, K)))
    loc_s2.wait()
    one_hot(sk2v[0, pl.ds(b // 4, 1), :], p2)
    ag1.got(18)
    ag1.go(21, 23)
    ag1.got(19)
    ag1.go(22, 24)
    ag1.got(9)
    ag1.go(12, 13)
    ag1.hand(1)
    ag1.got(10)
    ag1.go(14)
    ag1.hand(2)
    ag1.got(11)
    ag1.go(15)
    ag1.hand(3)
    ag1.got(0)
    ag1.go(3, 4)
    ag1.got(1)
    ag1.go(5)
    ag1.hand(10)
    ag1.got(2)
    ag1.go(6)
    ag1.hand(11)
    ag1.got(21)
    ag1.go(25)
    ag1.got(22)
    ag1.go(26)

    @pl.when(not_mid)
    def _():
        spread_side((1,), True)

    ag1.got(20)
    ag1.hand(9)
    ag1.got(12)
    ag1.go(16)
    ag1.hand(4)
    ag1.got(13)
    ag1.go(17)
    ag1.hand(5)

    @pl.when(not_mid)
    def _():
        spread_side((3,), False)

    t_w2i.start()
    t_w2o.start()
    ag1.got(3)
    ag1.go(7)
    ag1.got(4)
    ag1.go(8)

    ag1.got(23)
    ag1.hand(12)
    ag1.got(24)
    ag1.hand(13)
    ag1.together([14, 15])
    ag1.hand(6)
    ag1.together([16, 17])
    ag1.hand(7)

    @pl.when(not_mid)
    def _():
        spread_side((7, 5, 6, 4, 2), False)

    @pl.when(mid)
    def _():
        settle(ga.at[0, 2], dr1.at[0])
        sides = (base_of(endr, c, dp, 2) - times(lh2, ga, 2)).astype(BF)
        half = p2[pl.ds(pl.multiple_of(h * K, 16), K), :]
        stg[...] = fdot(sides, half).astype(BF).reshape(2, fr, K)
        t_pick.start()

    ag1.together([5, 6])
    ag1.hand(14)
    ag1.together([25, 26])
    ag1.together([7, 8])
    ag1.hand(15)

    @pl.when(not_mid)
    def _():
        settle(ga.at[0, 2], dr1.at[0])

    settle(ga.at[0, 0:2], dr1.at[1])

    into = srow.at[f // 4, :, pl.ds(pl.multiple_of(lw * (f % 4), 128), lw)]
    dest_box = b - c + 1 - h

    def pass_w2():
        t_w2i.wait_recv()
        t_w2fi.start()
        t_w2o.wait_recv()
        t_w2fo.start()

    def side_select():
        pltpu.make_async_copy(chunk_of(f), xs.at[own_rows, :], lsem.at[2]).wait()
        pltpu.make_async_copy(sib_chunk_of(f), xs.at[sib_rows, :], lsem.at[5]).wait()
        settle(xs.at[0 : 14 * fr, :], arecv.at[0])
        lane = lax.broadcasted_iota(jnp.int32, (K, 128), 1)
        mine = skt[...].astype(jnp.int32)
        total = None
        for part in range(8):
            hot = jnp.where(mine == lane + part * 128, 1.0, 0.0).astype(BF)
            term = fdot(hot, xs[part * 128 : (part + 1) * 128, :])
            total = term if total is None else total + term
        sel[...] = total.astype(BF)
        for d in (7, 5, 3, 1, 6, 4, 2, 0):
            rows = pl.ds(pl.multiple_of((f ^ d) * fr, 16), fr)
            remote(sel.at[rows, :], into, bsend.at[0], brecv.at[0], (dest_box, f ^ d)).start()

    def level_two():
        loc_w2.wait()
        t_w2.wait_recv()
        t_w2fi.wait_recv()
        t_w2fo.wait_recv()
        coupled(r2, h, lh, lh2, wb, p2, dp)

    def third(i):
        ag2.got(8 + 4 * i)
        ag2.go(10 + 4 * i)
        ag2.hand(2 * (8 + i))
        ag2.got(9 + 4 * i)
        ag2.go(11 + 4 * i)
        ag2.hand(2 * (4 + i))
        ag2.got(24 + 4 * i)
        ag2.go(26 + 4 * i)
        ag2.hand(2 * (4 * i + 1) + 1)
        ag2.got(25 + 4 * i)
        ag2.go(27 + 4 * i)
        ag2.hand(2 * (4 * i + 2) + 1)

    def finish(block):
        value = base_of(r2, h, dp, block) - times(lh2, gt, block)
        out[:, 0, :, block * K : (block + 1) * K] = value.astype(BF).reshape(2, fr, K)

    @pl.when(mid)
    def _():
        ends = fdot(lh2[...], ga[h, 0:2].reshape(2 * K, K))
        gt[h, 0:2, face_rows, :] = (-ends).astype(BF).reshape(2, fr, K)
        ag2.start(0)
        ag2.start(1)
        t_pick.wait_recv()
        gt[h, 2, face_rows, :] = stg[h] + pex[...]
        ag2.start(2)
        ag2.start(3)
        pass_w2()
        ag2.near(0)
        ag2.near(1)
        ag2.turn(0, 0)
        ag2.turn(1, 0)
        ag2.near(2)
        ag2.near(3)
        ag2.two_away(0)
        ag2.two_away(1)
        ag2.turn(2, 0)
        ag2.turn(3, 0)
        ag2.turn(0, 1)
        ag2.turn(1, 1)
        ag2.two_away(2)
        ag2.two_away(3)
        ag2.turn(0, 2)
        ag2.turn(1, 2)

        ag2.turn(2, 1)
        ag2.turn(3, 1)
        ag2.turn(0, 3)
        ag2.turn(1, 3)
        for i in (2, 3):
            ag2.turn(2, i)
            ag2.turn(3, i)
        settle(srow, brecv.at[0])
        seen = skt[face_rows, :]
        left1 = jnp.tile(jnp.where(seen < K, 1.0, 0.0), (1, 4)).astype(BF)
        right1 = 1 - left1
        left = jnp.concatenate([left1, left1], axis=0)
        right = 1 - left
        couple = [srow[t, :, K : 2 * K] * left1 + srow[t, :, 0:K] * right1 for t in range(2)]
        write_left(lhs_s, couple[0], couple[1])
        hid = fdot(lhs_s[...], wa[...].reshape(2 * K, K)).astype(BF)
        write_left(lh2_s, hid[:fr], hid[fr:])
        sides = srow[:, :, 2 * K :].reshape(2 * fr, K)
        dps[...] = (fdot(sides * left, p1[0:K, :]) + fdot(sides * right, p1[K:, :])).astype(BF)
        for block in (2, 0, 1):
            if block == 2:
                base = dps[...].astype(F32)
            else:
                on = left if block == 0 else right
                base = (srow[:, :, block * K : (block + 1) * K].reshape(2 * fr, K) * on).astype(F32)
            value = base - times(lh2_s, ga, block)
            r2[:, :, block * K : (block + 1) * K] = value.astype(BF).reshape(2, fr, K)

        level_two()
        ag2.corners(0)
        ag2.corners(1)
        ag2.last_corner(0)
        ag2.last_corner(1)
        finish(0)
        finish(1)
        ag2.corners(2)
        ag2.corners(3)
        ag2.last_corner(2)
        ag2.last_corner(3)

    @pl.when(not_mid)
    def _():
        for block in (2, 0, 1):
            value = base_of(endr, c, dp, block) - times(lh2, ga, block)
            r2[:, :, block * K : (block + 1) * K] = value.astype(BF).reshape(2, fr, K)
        pass_w2()
        side_select()
        level_two()
        settle(gt.at[:, 0:2], dr2.at[0])
        finish(0)
        finish(1)
        settle(gt.at[:, 2], dr2.at[1])

    finish(2)

    settle(ga.at[0, :, 0 : 7 * fr, :], ssem.at[0])
    settle(ga.at[0, :, 0 : 7 * fr, :], s1.at[0])
    settle(ga.at[0], ds1.at[0])

    @pl.when(mid)
    def _():
        settle(ga.at[0, 0, 0 : 7 * fr, :], ssem.at[1])
        settle(gt.at[:, :, 0 : K - fr // 2, :], s2.at[0])
        settle(gt, ds2.at[0])

    @pl.when(not_mid)
    def _():
        settle(sel, bsend.at[0])
        settle(xs.at[0 : 14 * fr, :], asend.at[0])


def on_device(leaf, w1, w2, skel1, skel2):
    fr = leaf.shape[4]
    hbm_spec = pl.BlockSpec(memory_space=pltpu.HBM)
    dma = pltpu.SemaphoreType.DMA
    lw = 3 * 2 * K // 8
    scratch = [
        pltpu.VMEM(skel1.shape, jnp.int32),
        pltpu.VMEM(skel2.shape, jnp.int32),
        pltpu.VMEM((2, fr, K), BF),
        pltpu.VMEM((2, fr, 3 * K), BF),
        pltpu.VMEM((2, fr, 3 * K), BF),
        pltpu.VMEM((2 * K, lw), BF),
        pltpu.VMEM((K, lw), BF),
        pltpu.VMEM((2, fr, 3 * K), BF),
        pltpu.VMEM((2 * K, K), BF),
        pltpu.VMEM((2 * K, K), BF),
        pltpu.VMEM((K, 128), F32),
        pltpu.VMEM((2, K, K), BF),
        pltpu.VMEM((2, K, K), BF),
        pltpu.VMEM((2, 3, K, K), BF),
        pltpu.VMEM((2, 3, K, K), BF),
        pltpu.VMEM((2 * fr, 2 * K), BF),
        pltpu.VMEM((2 * fr, 2 * K), BF),
        pltpu.VMEM((2 * fr, 2 * K), BF),
        pltpu.VMEM((2 * fr, 2 * K), BF),
        pltpu.VMEM((2 * fr, K), BF),
        pltpu.VMEM((2 * fr, K), BF),
        pltpu.VMEM((2, fr, 3 * K), BF),
        pltpu.VMEM((2, fr, K), BF),
        pltpu.VMEM((fr, K), BF),
        dma((8,)),
        dma((2,)),
        dma((9,)),
        dma((1,)),
        dma((22,)),
        dma((1,)),
        dma((2,)),
        dma((1,)),
        dma((52,)),
        dma((1,)),
        dma((2,)),
        dma((1,)),
        dma((1,)),
        dma((1,)),
        dma((1,)),
    ]
    return pl.pallas_call(
        functools.partial(kernel, fr),
        out_shape=jax.ShapeDtypeStruct((2, 1, fr, 3 * K), BF),
        in_specs=[hbm_spec] * 5,
        out_specs=pl.BlockSpec(memory_space=pltpu.VMEM),
        scratch_shapes=scratch,
        compiler_params=pltpu.CompilerParams(
            collective_id=0, has_side_effects=True, vmem_limit_bytes=GRANT
        ),
    )(*[pltpu.with_memory_space_constraint(a, pltpu.HBM) for a in (leaf, w1, w2, skel1, skel2)])


def solution(mesh):
    return jax.shard_map(
        on_device,
        mesh=mesh,
        in_specs=(
            P(None, None, "box", None, "face", None),
            P(None, None, "box", None),
            P(None, None, "box", None),
            P(),
            P(),
        ),
        out_specs=P(None, None, ("box", "face"), None),
        check_vma=False,
    )
```

```python
import functools

import jax
import jax.numpy as jnp
from jax import lax
from jax.experimental import pallas as pl
from jax.experimental.pallas import tpu as pltpu
from jax.sharding import PartitionSpec as P

K = 512
BF = jnp.bfloat16
F32 = jnp.float32
MESH = pl.DeviceIdType.MESH
GRANT = 48 * 1024 * 1024


def fdot(a, b):
    return jnp.dot(a, b, preferred_element_type=F32)


def remote(src, dst, send, recv, target):
    return pltpu.make_async_remote_copy(
        src_ref=src, dst_ref=dst, send_sem=send, recv_sem=recv, device_id=target, device_id_type=MESH
    )


def write_left(ref, real, imag):
    n = real.shape[0]
    ref[0:n, 0:K] = real
    ref[0:n, K : 2 * K] = -imag
    ref[n : 2 * n, 0:K] = imag
    ref[n : 2 * n, K : 2 * K] = real


class Gather:
    def __init__(self, view, send, recv, dsend, drecv, sib):
        self.view, self.send, self.recv, self.dsend, self.drecv, self.sib = view, send, recv, dsend, drecv, sib
        self.hops, self.hands, self.split, self.shared = [], [], 8, []

    def hop(self, k):
        what, to = self.hops[k]
        ref = self.view(*what)
        return remote(ref, ref, self.send.at[0], self.recv.at[self.sem_of(k)], to)

    def together(self, slots):
        settle(self.same_bytes(slots, len(slots)), self.recv.at[self.sem_of(slots[0])])

    def hand_over(self, k):
        ref = self.view(*self.hands[k])
        return remote(ref, ref, self.dsend.at[0], self.drecv.at[k // self.split], self.sib)

    def sem_of(self, k):
        first = {slot: group[0] for group in self.shared for slot in group}
        used = [slot for slot in range(len(self.hops)) if first.get(slot, slot) == slot]
        return used.index(first.get(k, k))

    def got(self, *ks):
        for k in ks:
            self.hop(k).wait_recv()

    def go(self, *ks):
        for k in ks:
            self.hop(k).start()

    def hand(self, *ks):
        for k in ks:
            self.hand_over(k).start()


def settle(view, sem):
    pltpu.make_async_copy(view, view, sem).wait()


def face_gather(view, sems, b, f, c, sib):
    g = Gather(view, *sems, sib)
    y, xh = f // 2, f % 2

    def at(dy, dx):
        return (c, ((y + dy) % 4) * 2 + (xh + dx) % 2)

    own, up, down, far = at(0, 0), at(1, 0), at(3, 0), at(2, 0)
    side, up_side, down_side, far_side = at(0, 1), at(1, 1), at(3, 1), at(2, 1)
    lo, hi, full = (0, K // 2), (K // 2, K // 2), (0, K)
    x, u, d = (b, side[1]), (b, up[1]), (b, down[1])
    for piece in ((0, 1), (2, 1)):
        g.hops += [
            ((own, piece, full), x),
            ((own, piece, full), u),
            ((own, piece, full), d),
            ((side, piece, full), u),
            ((side, piece, full), d),
            ((down, piece, lo), u),
            ((up, piece, hi), d),
            ((down_side, piece, lo), u),
            ((up_side, piece, hi), d),
        ]
    piece = (1, 1)
    g.hops += [
        ((own, piece, full), u),
        ((own, piece, full), d),
        ((own, piece, full), x),
        ((down, piece, lo), u),
        ((up, piece, hi), d),
        ((down, piece, full), x),
        ((up, piece, full), x),
        ((far, piece, lo), x),
        ((far, piece, hi), x),
    ]
    ends, picked = (0, 2), (2, 1)
    places = (own, side, down, up, down_side, up_side, far, far_side)
    g.shared = [[5, 6], [7, 8], [14, 15], [16, 17], [25, 26]]
    g.hands = [(place, picked, full) for place in places] + [(place, ends, full) for place in places]
    return g


class Plane(Gather):
    def __init__(self, view, sems, b, f, h, cross_box, sib, fr):
        super().__init__(view, *sems, sib)
        self.split = 32
        y, xh = f // 2, f % 2

        def face(dy, dx):
            return ((y + dy) % 4) * 2 + (xh + dx) % 2

        xs = [(h, 0), (1 - h, 0), (1 - h, 1), (h, 1)]
        ys = [0, 1, 3, 2]

        def node(iy, ix):
            return (xs[ix][0], face(ys[iy], xs[ix][1]))

        lo, hi, full = (0, K // 2), (K // 2, K // 2), (0, K)
        inner, outer = (cross_box, f), (cross_box, face(0, 1))
        up, down = (b, face(1, 0)), (b, face(3, 0))
        for p, piece in enumerate(((0, 0, fr), (1, 0, fr), (2, 0, fr // 2), (2, fr // 2, fr // 2))):

            def line_x():
                return [(own, inner), (own, outer), (own, (b, face(0, 1)))]

            def line_y():
                return [(own, up), (own, down), (own, (b, face(2, 0)))]

            def round_x(iy):
                return [
                    ((node(iy, 0), piece, full), inner),
                    ((node(iy, 0), piece, full), outer),
                    ((node(iy, 1), piece, lo), outer),
                    ((node(iy, 2), piece, hi), inner),
                ]

            def round_y(ix):
                return [
                    ((node(0, ix), piece, full), up),
                    ((node(0, ix), piece, full), down),
                    ((node(2, ix), piece, lo), up),
                    ((node(1, ix), piece, hi), down),
                ]

            own = (node(0, 0), piece, full)
            first, second = (line_x, round_y) if p % 2 == 0 else (line_y, round_x)
            self.hops += first()
            for i in range(4):
                self.hops += second(i)
            self.hands += [(node(i // 4, i % 4), piece, full) for i in range(16)]
            k = 19 * p + 5
            self.shared += [[k, k + 1, k + 4, k + 5, k + 8, k + 9], [k + 12, k + 13]]

    def give(self, p, along, across):
        iy, ix = (across, along) if p % 2 == 0 else (along, across)
        self.hand(16 * p + 4 * iy + ix)

    def start(self, p):
        k = 19 * p
        self.go(k, k + 1, k + 2, k + 3, k + 4)
        self.give(p, 0, 0)

    def near(self, p):
        k = 19 * p
        for slot in (0, 1):
            place = 1 + slot if p % 2 == 0 else 2 - slot
            self.got(k + slot)
            self.go(k + 3 + 4 * place, k + 4 + 4 * place)
            self.give(p, place, 0)

    def two_away(self, p):
        k = 19 * p
        self.got(k + 2)
        self.go(k + 15, k + 16)
        self.give(p, 3, 0)

    def turn(self, p, i):
        k = 19 * p + 3 + 4 * i
        for slot in (0, 1):
            self.got(k + slot)
            self.go(k + 2 + slot)
            self.give(p, i, 2 - slot if p % 2 == 0 else 1 + slot)

    def corners(self, p):
        k = 19 * p + 5
        self.together([k, k + 1, k + 4, k + 5, k + 8, k + 9])
        for i in range(3):
            self.give(p, i, 3)

    def last_corner(self, p):
        k = 19 * p + 17
        self.together([k, k + 1])
        self.give(p, 3, 3)


def kernel(fr, leaf, w1, w2, skel1, skel2, out, sk1v, sk2v, ifs, endr, sraw, xs, sel, srow, p1, p2, skt, wa, wb, ga, gt,
           lh, lh2, lhs_s, lh2_s, dp, dps, r2, stg, pex, lsem, ssem, rsem, s1, r1, ds1, dr1, s2, r2s, ds2, dr2,
           asend, arecv, bsend, brecv):
    b, f = lax.axis_index("box"), lax.axis_index("face")
    c, h = b % 2, (b // 2) % 2
    q = b % 4
    sib = (b + 1 - 2 * c, f)
    inner_box = b + 2 - 4 * h
    other_face = f // 2 * 2 + 1 - f % 2
    inner, outer = (inner_box, f), (inner_box, other_face)
    cross_box = inner_box + 1 - 2 * c
    mid = c != h
    not_mid = jnp.logical_not(mid)

    barrier = pltpu.get_barrier_semaphore()
    up, down = (f + 2) % 8, (f + 6) % 8
    peers = [(b, up), (b, down), (b, other_face), sib, inner, outer, (cross_box, f), (cross_box, other_face)]
    for peer in peers:
        pl.semaphore_signal(barrier, inc=1, device_id=peer, device_id_type=MESH)

    def local(k, src, dst):
        copy = pltpu.make_async_copy(src, dst, lsem.at[k])
        copy.start()
        return copy

    loc_s1 = local(5, skel1, sk1v)
    loc_s2 = local(6, skel2, sk2v)
    lw = 3 * 2 * K // 8
    face_rows = pl.ds(pl.multiple_of(f * fr, 16), fr)
    own_rows = pl.ds(pl.multiple_of(c * K + f * fr, 16), fr)
    own_cols = pl.ds(pl.multiple_of(c * K, 128), K)
    loc_ga = local(7, leaf.at[:, 0, 0, 1 - c, :, own_cols], ga.at[c, 0:2, face_rows, :])
    loc_if = local(0, leaf.at[c, 0, 0, 1 - c, :, 2 * K : 3 * K], ifs.at[c])
    loc_end = local(1, leaf.at[:, 0, 0, c], endr)

    def chunk_of(j):
        return leaf.at[j // 4, 0, 0, 2, :, pl.ds(pl.multiple_of(lw * (j % 4), 128), lw)]


    @pl.when(not_mid)
    def _():
        pltpu.make_async_copy(chunk_of(f), xs.at[own_rows, :], lsem.at[2]).start()

    sib_rows = pl.ds(pl.multiple_of((1 - c) * K + f * fr, 16), fr)

    w1_rows = pl.ds(pl.multiple_of(c * (K // 2), 16), K // 2)
    w2_rows = pl.ds(pl.multiple_of(q * (K // 4), 16), K // 4)
    loc_w1 = local(3, w1.at[:, 0], wa.at[:, w1_rows, :])
    loc_w2 = local(4, w2.at[:, 0], wb.at[:, w2_rows, :])

    loc_ga.wait()

    pl.semaphore_wait(barrier, len(peers))

    t_if = remote(leaf.at[1 - c, 0, 0, 1 - c, :, 2 * K : 3 * K], ifs.at[c], ssem.at[0], rsem.at[0], sib)
    t_w1 = remote(w1.at[:, 0], wa.at[:, w1_rows, :], ssem.at[0], rsem.at[1], sib)
    t_w2 = remote(w2.at[:, 0], wb.at[:, w2_rows, :], ssem.at[0], rsem.at[2], sib)
    t_w2i = remote(w2.at[0, 0], wb.at[0, w2_rows, :], ssem.at[0], rsem.at[3], inner)
    t_w2o = remote(w2.at[1, 0], wb.at[1, w2_rows, :], ssem.at[0], rsem.at[4], outer)
    q2 = pl.ds(pl.multiple_of((q + 2 - 4 * h) * (K // 4), 16), K // 4)
    t_w2fi = remote(wb.at[0, q2, :], wb.at[0, q2, :], ssem.at[0], rsem.at[5], sib)
    t_w2fo = remote(wb.at[1, q2, :], wb.at[1, q2, :], ssem.at[0], rsem.at[6], sib)
    t_side = remote(leaf.at[:, 0, 0, 2], sraw, ssem.at[1], rsem.at[7], sib)
    t_pick = remote(stg.at[1 - h], pex, ssem.at[1], rsem.at[8], (cross_box, f))
    picker_box = b - c + h

    def sib_chunk_of(j):
        return sraw.at[j // 4, :, pl.ds(pl.multiple_of(lw * (j % 4), 128), lw)]

    def spread_side(places, first):
        if first:
            t_side.wait_recv()
            pltpu.make_async_copy(sib_chunk_of(f), xs.at[sib_rows, :], lsem.at[5]).start()
        for d in places:
            to = (picker_box, f ^ d)
            remote(chunk_of(f ^ d), xs.at[own_rows, :], asend.at[0], arecv.at[0], to).start()
            remote(sib_chunk_of(f ^ d), xs.at[sib_rows, :], asend.at[0], arecv.at[0], to).start()

    def part_rows(node, blocks, cols):
        rows = pl.ds(pl.multiple_of(node[1] * fr, 16), fr)
        return ga.at[node[0], blocks[0] : blocks[0] + blocks[1], rows, cols[0] : cols[0] + cols[1]]

    def plane_rows(node, piece, cols):
        block, at, n = piece
        return gt.at[node[0], block, pl.ds(pl.multiple_of(node[1] * fr + at, 16), n), cols[0] : cols[0] + cols[1]]

    def half_ga(slots, n):
        return ga.at[0, 0, 0 : n * fr // 2, :]

    def half_gt(slots, n):
        rows = fr if slots[0] < 38 else fr // 2
        return gt.at[0, 0, 0 : n * rows // 2, :]

    ag1 = face_gather(part_rows, (s1, r1, ds1, dr1), b, f, c, sib)
    ag2 = Plane(plane_rows, (s2, r2s, ds2, dr2), b, f, h, cross_box, sib, fr)
    ag1.same_bytes, ag2.same_bytes = half_ga, half_gt

    t_if.start()
    ag1.go(18, 19, 0)
    ag1.hand(8)
    t_w1.start()
    t_w2.start()

    @pl.when(mid)
    def _():
        t_side.start()


    def one_hot(rows, pick):
        for part in range(4):
            at = part * 256
            index = lax.broadcasted_iota(jnp.int32, (256, K), 0) + at
            pick[at : at + 256, :] = jnp.where(index == rows, 1.0, 0.0).astype(BF)

    loc_s1.wait()
    sk1 = sk1v[0, pl.ds(b // 2, 1), :]
    one_hot(sk1, p1)
    loc_if.wait()
    t_if.wait_recv()
    ga[c, 2, face_rows, :] = (fdot(ifs[0], p1[0:K, :]) + fdot(ifs[1], p1[K:, :])).astype(BF)
    ag1.go(9, 10, 11, 1, 2, 20)
    ag1.hand(0)

    def coupled(rows, side, left, left2, weights, pick, dest):
        couple = rows[:, :, pl.ds(pl.multiple_of((1 - side) * K, 128), K)]
        write_left(left, couple[0], couple[1])
        hid = fdot(left[...], weights[...].reshape(2 * K, K)).astype(BF)
        write_left(left2, hid[:fr], hid[fr:])
        side_cols = rows[:, :, 2 * K :].reshape(2 * fr, K)
        half = pick[pl.ds(pl.multiple_of(side * K, 16), K), :]
        dest[...] = fdot(side_cols, half).astype(BF)

    def base_of(rows, side, dest, block):
        if block == 2:
            return dest[...].astype(F32)
        on = jnp.where(side == block, 1.0, 0.0)
        return rows[:, :, block * K : (block + 1) * K].reshape(2 * fr, K).astype(F32) * on

    def times(left2, gathered, block):
        if block == 2:
            left = left2[...]
            return fdot(left[:, :K], gathered[0, 2]) + fdot(left[:, K:], gathered[1, 2])
        return fdot(left2[...], gathered[block, 0:2].reshape(2 * K, K))

    loc_end.wait()
    loc_w1.wait()
    t_w1.wait_recv()
    coupled(endr, c, lh, lh2, wa, p1, dp)

    skt[...] = jnp.transpose(jnp.broadcast_to(sk1.astype(F32), (128, K)))
    loc_s2.wait()
    one_hot(sk2v[0, pl.ds(b // 4, 1), :], p2)
    ag1.got(18)
    ag1.go(21, 23)
    ag1.got(19)
    ag1.go(22, 24)
    ag1.got(9)
    ag1.go(12, 13)
    ag1.hand(1)
    ag1.got(10)
    ag1.go(14)
    ag1.hand(2)
    ag1.got(11)
    ag1.go(15)
    ag1.hand(3)
    ag1.got(0)
    ag1.go(3, 4)
    ag1.got(1)
    ag1.go(5)
    ag1.hand(10)
    ag1.got(2)
    ag1.go(6)
    ag1.hand(11)
    ag1.got(21)
    ag1.go(25)
    ag1.got(22)
    ag1.go(26)

    @pl.when(not_mid)
    def _():
        spread_side((1,), True)

    ag1.got(20)
    ag1.hand(9)
    ag1.got(12)
    ag1.go(16)
    ag1.hand(4)
    ag1.got(13)
    ag1.go(17)
    ag1.hand(5)

    @pl.when(not_mid)
    def _():
        spread_side((3,), False)

    t_w2i.start()
    t_w2o.start()
    ag1.got(3)
    ag1.go(7)
    ag1.got(4)
    ag1.go(8)

    @pl.when(not_mid)
    def _():
        spread_side((6, 4, 2), False)


    ag1.got(23)
    ag1.hand(12)
    ag1.got(24)
    ag1.hand(13)
    ag1.together([14, 15])
    ag1.hand(6)
    ag1.together([16, 17])
    ag1.hand(7)

    @pl.when(not_mid)
    def _():
        spread_side((7, 5), False)

    @pl.when(mid)
    def _():
        settle(ga.at[0, 2], dr1.at[0])
        sides = (base_of(endr, c, dp, 2) - times(lh2, ga, 2)).astype(BF)
        half = p2[pl.ds(pl.multiple_of(h * K, 16), K), :]
        stg[...] = fdot(sides, half).astype(BF).reshape(2, fr, K)
        t_pick.start()

    ag1.together([5, 6])
    ag1.hand(14)
    ag1.together([25, 26])
    ag1.together([7, 8])
    ag1.hand(15)

    @pl.when(not_mid)
    def _():
        settle(ga.at[0, 2], dr1.at[0])

    settle(ga.at[0, 0:2], dr1.at[1])

    into = srow.at[f // 4, :, pl.ds(pl.multiple_of(lw * (f % 4), 128), lw)]
    dest_box = b - c + 1 - h

    def pass_w2():
        t_w2i.wait_recv()
        t_w2fi.start()
        t_w2o.wait_recv()
        t_w2fo.start()

    def side_select():
        pltpu.make_async_copy(chunk_of(f), xs.at[own_rows, :], lsem.at[2]).wait()
        pltpu.make_async_copy(sib_chunk_of(f), xs.at[sib_rows, :], lsem.at[5]).wait()
        settle(xs.at[0 : 14 * fr, :], arecv.at[0])
        lane = lax.broadcasted_iota(jnp.int32, (K, 128), 1)
        mine = skt[...].astype(jnp.int32)
        total = None
        for part in range(8):
            hot = jnp.where(mine == lane + part * 128, 1.0, 0.0).astype(BF)
            term = fdot(hot, xs[part * 128 : (part + 1) * 128, :])
            total = term if total is None else total + term
        sel[...] = total.astype(BF)
        for d in (7, 5, 3, 1, 6, 4, 2, 0):
            rows = pl.ds(pl.multiple_of((f ^ d) * fr, 16), fr)
            remote(sel.at[rows, :], into, bsend.at[0], brecv.at[0], (dest_box, f ^ d)).start()

    def level_two():
        loc_w2.wait()
        t_w2.wait_recv()
        t_w2fi.wait_recv()
        t_w2fo.wait_recv()
        coupled(r2, h, lh, lh2, wb, p2, dp)

    def third(i):
        ag2.got(8 + 4 * i)
        ag2.go(10 + 4 * i)
        ag2.hand(2 * (8 + i))
        ag2.got(9 + 4 * i)
        ag2.go(11 + 4 * i)
        ag2.hand(2 * (4 + i))
        ag2.got(24 + 4 * i)
        ag2.go(26 + 4 * i)
        ag2.hand(2 * (4 * i + 1) + 1)
        ag2.got(25 + 4 * i)
        ag2.go(27 + 4 * i)
        ag2.hand(2 * (4 * i + 2) + 1)

    def finish(block):
        value = base_of(r2, h, dp, block) - times(lh2, gt, block)
        out[:, 0, :, block * K : (block + 1) * K] = value.astype(BF).reshape(2, fr, K)

    @pl.when(mid)
    def _():
        ends = fdot(lh2[...], ga[h, 0:2].reshape(2 * K, K))
        gt[h, 0:2, face_rows, :] = (-ends).astype(BF).reshape(2, fr, K)
        ag2.start(0)
        ag2.start(1)
        t_pick.wait_recv()
        gt[h, 2, face_rows, :] = stg[h] + pex[...]
        ag2.start(2)
        ag2.start(3)
        pass_w2()
        ag2.near(0)
        ag2.near(1)
        ag2.turn(0, 0)
        ag2.turn(1, 0)
        ag2.near(2)
        ag2.near(3)
        ag2.two_away(0)
        ag2.two_away(1)
        ag2.turn(2, 0)
        ag2.turn(3, 0)
        ag2.turn(0, 1)
        ag2.turn(1, 1)
        ag2.two_away(2)
        ag2.two_away(3)
        ag2.turn(0, 2)
        ag2.turn(1, 2)

        ag2.turn(2, 1)
        ag2.turn(3, 1)
        ag2.turn(0, 3)
        ag2.turn(1, 3)
        for i in (2, 3):
            ag2.turn(2, i)
            ag2.turn(3, i)
        settle(srow, brecv.at[0])
        seen = skt[face_rows, :]
        left1 = jnp.tile(jnp.where(seen < K, 1.0, 0.0), (1, 4)).astype(BF)
        right1 = 1 - left1
        left = jnp.concatenate([left1, left1], axis=0)
        right = 1 - left
        couple = [srow[t, :, K : 2 * K] * left1 + srow[t, :, 0:K] * right1 for t in range(2)]
        write_left(lhs_s, couple[0], couple[1])
        hid = fdot(lhs_s[...], wa[...].reshape(2 * K, K)).astype(BF)
        write_left(lh2_s, hid[:fr], hid[fr:])
        sides = srow[:, :, 2 * K :].reshape(2 * fr, K)
        dps[...] = (fdot(sides * left, p1[0:K, :]) + fdot(sides * right, p1[K:, :])).astype(BF)
        for block in (2, 0, 1):
            if block == 2:
                base = dps[...].astype(F32)
            else:
                on = left if block == 0 else right
                base = (srow[:, :, block * K : (block + 1) * K].reshape(2 * fr, K) * on).astype(F32)
            value = base - times(lh2_s, ga, block)
            r2[:, :, block * K : (block + 1) * K] = value.astype(BF).reshape(2, fr, K)

        level_two()
        ag2.corners(0)
        ag2.corners(1)
        ag2.last_corner(0)
        ag2.last_corner(1)
        finish(0)
        finish(1)
        ag2.corners(2)
        ag2.corners(3)
        ag2.last_corner(2)
        ag2.last_corner(3)

    @pl.when(not_mid)
    def _():
        for block in (2, 0, 1):
            value = base_of(endr, c, dp, block) - times(lh2, ga, block)
            r2[:, :, block * K : (block + 1) * K] = value.astype(BF).reshape(2, fr, K)
        pass_w2()
        side_select()
        level_two()
        settle(gt.at[:, 0:2], dr2.at[0])
        finish(0)
        finish(1)
        settle(gt.at[:, 2], dr2.at[1])

    finish(2)

    settle(ga.at[0, :, 0 : 7 * fr, :], ssem.at[0])
    settle(ga.at[0, :, 0 : 7 * fr, :], s1.at[0])
    settle(ga.at[0], ds1.at[0])

    @pl.when(mid)
    def _():
        settle(ga.at[0, 0, 0 : 7 * fr, :], ssem.at[1])
        settle(gt.at[:, :, 0 : K - fr // 2, :], s2.at[0])
        settle(gt, ds2.at[0])

    @pl.when(not_mid)
    def _():
        settle(sel, bsend.at[0])
        settle(xs.at[0 : 14 * fr, :], asend.at[0])


def on_device(leaf, w1, w2, skel1, skel2):
    fr = leaf.shape[4]
    hbm_spec = pl.BlockSpec(memory_space=pltpu.HBM)
    dma = pltpu.SemaphoreType.DMA
    lw = 3 * 2 * K // 8
    scratch = [
        pltpu.VMEM(skel1.shape, jnp.int32),
        pltpu.VMEM(skel2.shape, jnp.int32),
        pltpu.VMEM((2, fr, K), BF),
        pltpu.VMEM((2, fr, 3 * K), BF),
        pltpu.VMEM((2, fr, 3 * K), BF),
        pltpu.VMEM((2 * K, lw), BF),
        pltpu.VMEM((K, lw), BF),
        pltpu.VMEM((2, fr, 3 * K), BF),
        pltpu.VMEM((2 * K, K), BF),
        pltpu.VMEM((2 * K, K), BF),
        pltpu.VMEM((K, 128), F32),
        pltpu.VMEM((2, K, K), BF),
        pltpu.VMEM((2, K, K), BF),
        pltpu.VMEM((2, 3, K, K), BF),
        pltpu.VMEM((2, 3, K, K), BF),
        pltpu.VMEM((2 * fr, 2 * K), BF),
        pltpu.VMEM((2 * fr, 2 * K), BF),
        pltpu.VMEM((2 * fr, 2 * K), BF),
        pltpu.VMEM((2 * fr, 2 * K), BF),
        pltpu.VMEM((2 * fr, K), BF),
        pltpu.VMEM((2 * fr, K), BF),
        pltpu.VMEM((2, fr, 3 * K), BF),
        pltpu.VMEM((2, fr, K), BF),
        pltpu.VMEM((fr, K), BF),
        dma((8,)),
        dma((2,)),
        dma((9,)),
        dma((1,)),
        dma((22,)),
        dma((1,)),
        dma((2,)),
        dma((1,)),
        dma((52,)),
        dma((1,)),
        dma((2,)),
        dma((1,)),
        dma((1,)),
        dma((1,)),
        dma((1,)),
    ]
    return pl.pallas_call(
        functools.partial(kernel, fr),
        out_shape=jax.ShapeDtypeStruct((2, 1, fr, 3 * K), BF),
        in_specs=[hbm_spec] * 5,
        out_specs=pl.BlockSpec(memory_space=pltpu.VMEM),
        scratch_shapes=scratch,
        compiler_params=pltpu.CompilerParams(
            collective_id=0, has_side_effects=True, vmem_limit_bytes=GRANT
        ),
    )(*[pltpu.with_memory_space_constraint(a, pltpu.HBM) for a in (leaf, w1, w2, skel1, skel2)])


def solution(mesh):
    return jax.shard_map(
        on_device,
        mesh=mesh,
        in_specs=(
            P(None, None, "box", None, "face", None),
            P(None, None, "box", None),
            P(None, None, "box", None),
            P(),
            P(),
        ),
        out_specs=P(None, None, ("box", "face"), None),
        check_vma=False,
    )
```
